32 devices in a mesh: seq: 16 (over z, y, x), head: 2 (over core).
Axes of the slice: x: 2, y: 2, z: 4, core: 2. Of those that a mesh axis runs over, the one named last changes fastest.
Arguments:
- queries: bfloat16 [4096, 4096], P('seq', 'head'), may hold values from -1.796875 to 1.796875
- key_rows: bfloat16 [4096, 4096], P('seq', 'head'), may hold values from -1.796875 to 1.796875
- values: bfloat16 [4096, 4096], P('seq', 'head'), may hold values from -100 to 100
- out_weight: bfloat16 [4096, 4096], P('head', 'seq'), may hold values from -0.125 to 0.125
- out_grad: bfloat16 [4096, 4096], P('seq', 'head'), may hold values from -6 to 6
Outputs:
- mixed: bfloat16 [4096, 4096], P('seq', 'head')
- query_grad: bfloat16 [4096, 4096], P('seq', 'head')
- key_grad: bfloat16 [4096, 4096], P('seq', 'head')
- value_grad: bfloat16 [4096, 4096], P('seq', 'head')
The draws below stay inside these ranges and needn't reach their ends.
All inputs are finite; a program needn't handle non-finite values.
Results may differ from the reference program's by a relative error of at most 0.014.
Values may be sent and summed in bfloat16 or wider, within the bound.
A program may use at most 128 MiB of HBM per device.

```python
import math
import jax
import jax.numpy as jnp
from jax import lax

D = 4096
HEADS = 32
HEAD_DIM = 128
TOK_DEV = 256
TOKENS = 4096
INNER = 4096
N_HEAD = 2


def draw_values(key, part):
    row_key = jax.random.fold_in(key, 11)
    col_key = jax.random.fold_in(key, 12)
    entry_key = jax.random.fold_in(key, 13)
    row_scale = jnp.exp(jax.random.uniform(row_key, (TOKENS, 1), jnp.float32) * math.log(10.0))
    col_scale = jnp.exp(jax.random.uniform(col_key, (1, INNER), jnp.float32) * math.log(10.0))
    entries = jnp.clip(jax.random.normal(entry_key, (TOKENS, INNER), jnp.float32), -4.0, 4.0)
    return (entries * row_scale * col_scale / 4.0).astype(jnp.bfloat16)


def with_spikes(drawn, stream_key, source, target, shards_of, factor):
    owner, partner = [(jnp.arange(drawn.shape[axis_at]) // (drawn.shape[axis_at] // shards_of)).reshape([-1 if axis == axis_at else 1 for axis in range(drawn.ndim)]) for axis_at in (source, target)]
    chosen = jax.random.permutation(stream_key, shards_of)[partner]
    strong = (owner == chosen) | (owner == (partner + shards_of // 2) % shards_of)
    return jnp.where(strong, factor * drawn, drawn)


def block_scale(key, dims, split, low, high):
    def one(position, blocks):
        steps = jax.random.uniform(jax.random.fold_in(jax.random.fold_in(key, 6), position), (blocks,), jnp.float32, low / len(split), high / len(split))
        return jnp.repeat(jnp.exp(steps), dims[position] // blocks).reshape((-1,) + (1,) * (len(dims) - position - 1))

    loudness = one(*split[0])
    for cut in split[1:]:
        loudness = loudness * one(*cut)
    return loudness


def gaussian(key, extent, width, reach, shards=(), kind=jnp.bfloat16):
    gain = block_scale(key, extent, shards, -0.22, 0.18) if shards else 1.0
    array = jax.random.normal(key, extent, jnp.float32) * width * gain
    return jnp.minimum(jnp.maximum(array, -reach), reach).astype(kind)


def heavy_noise(rng, dims, width, reach, pieces, heavy, dtype=jnp.bfloat16):
    array = width * jax.random.normal(rng, dims, jnp.float32)
    if pieces:
        array = array * block_scale(rng, dims, pieces, -0.22, 0.18)
    return jnp.clip(with_spikes(array, jax.random.fold_in(rng, 3), *heavy), -reach, reach).astype(dtype)


def setup_inputs(seed: int = 0) -> dict:
    streams_of = jax.random.split(jax.random.key(seed), 6)
    return {
        "queries": gaussian(streams_of[0], (TOKENS, INNER), 0.3, 1.796875, ((0, 16), (1, 2))),
        "key_rows": gaussian(streams_of[1], (TOKENS, INNER), 0.3, 1.796875, ((0, 16), (1, 2))),
        "values": draw_values(jax.random.fold_in(streams_of[5], 71), 0),
        "out_weight": heavy_noise(streams_of[3], (INNER, D), INNER ** -0.5, 0.125, ((0, 2), (1, 16)), (0, 1, 16, 2.0)),
        "out_grad": gaussian(streams_of[4], (TOKENS, D), 1.0, 6.0, ((0, 16), (1, 2))),
    }


def rounded(tensor):
    return lax.optimization_barrier(tensor.astype(jnp.bfloat16)).astype(jnp.float32)

def lower_mask(length):
    row_ids = lax.broadcasted_iota(jnp.int32, (length, length), 0)
    col_ids = lax.broadcasted_iota(jnp.int32, (length, length), 1)
    return row_ids >= col_ids

def reference(queries, key_rows, values, out_weight, out_grad):
    block_count = TOKENS // TOK_DEV
    head_shape = (block_count, TOK_DEV, HEADS, HEAD_DIM)
    query_blocks = queries.reshape(head_shape)
    key_blocks = key_rows.reshape(head_shape)
    value_blocks = values.reshape(head_shape)
    grad_blocks = out_grad.reshape(block_count, TOK_DEV, D)
    causal = lower_mask(TOK_DEV)[None]
    group_width = INNER // N_HEAD

    def state_of(packed):
        key_part, value_part = packed
        return jnp.einsum('shd,she->hde', key_part.astype(jnp.float32), value_part.astype(jnp.float32))
    local_state = lax.map(state_of, (key_blocks, value_blocks))
    running_state = jnp.cumsum(local_state, axis=0)
    prefix_state = jnp.concatenate([jnp.zeros_like(local_state[:1]), running_state[:-1]], axis=0)

    def forward(packed):
        query_part, key_part, value_part, prefix_part, grad_part = packed
        query_wide = query_part.astype(jnp.float32)
        key_wide = key_part.astype(jnp.float32)
        value_wide = value_part.astype(jnp.float32)
        scores = jnp.einsum('thd,shd->hts', query_wide, key_wide)
        weights = rounded(jnp.where(causal, scores, 0.0))
        numerator = jnp.einsum('hts,she->the', weights, value_wide) + jnp.einsum('thd,hde->the', query_wide, rounded(prefix_part))
        spread = jnp.sqrt(lax.optimization_barrier(jnp.mean(numerator * numerator, axis=-1, keepdims=True)) + 1e-06)
        normed = numerator / spread
        attended = normed.astype(jnp.bfloat16).reshape(TOK_DEV, INNER)
        summed = jnp.zeros((TOK_DEV, D), jnp.float32)
        for group in range(N_HEAD):
            first_col = group * group_width
            term = jnp.dot(attended[:, first_col:first_col + group_width], out_weight[first_col:first_col + group_width], preferred_element_type=jnp.float32)
            summed = summed + rounded(term)
        layer_out = summed.astype(jnp.bfloat16)
        out_dir = lax.dot_general(grad_part, out_weight, (((1,), (1,)), ((), ())), preferred_element_type=jnp.float32)
        out_dir = out_dir.reshape(TOK_DEV, HEADS, HEAD_DIM)
        along_dir = lax.optimization_barrier(jnp.mean(out_dir * normed, axis=-1, keepdims=True))
        numer_grad = rounded((out_dir - normed * along_dir) / spread)
        local_grad = jnp.einsum('thd,the->hde', query_wide, numer_grad)
        return (layer_out, numer_grad, local_grad)
    layer_out, numer_grad, local_grad = lax.map(forward, (query_blocks, key_blocks, value_blocks, prefix_state, grad_blocks))
    reversed_sum = jnp.cumsum(local_grad[::-1], axis=0)[::-1]
    suffix_grad = jnp.concatenate([reversed_sum[1:], jnp.zeros_like(local_grad[:1])], axis=0)

    def backward(packed):
        query_part, key_part, value_part, prefix_part, suffix_part, numer_part = packed
        query_wide = query_part.astype(jnp.float32)
        key_wide = key_part.astype(jnp.float32)
        value_wide = value_part.astype(jnp.float32)
        scores = jnp.einsum('thd,shd->hts', query_wide, key_wide)
        weights = rounded(jnp.where(causal, scores, 0.0))
        pair_scores = jnp.einsum('the,she->hts', numer_part, value_wide)
        pair_low = rounded(jnp.where(causal, pair_scores, 0.0))
        prefix_low = rounded(prefix_part)
        suffix_low = rounded(suffix_part)
        query_out = jnp.einsum('hts,shd->thd', pair_low, key_wide) + jnp.einsum('the,hde->thd', numer_part, prefix_low)
        key_out = jnp.einsum('hts,thd->shd', pair_low, query_wide) + jnp.einsum('she,hde->shd', value_wide, suffix_low)
        value_out = jnp.einsum('hts,the->she', weights, numer_part) + jnp.einsum('shd,hde->she', key_wide, suffix_low)
        flat_shape = (TOK_DEV, INNER)
        return (query_out.reshape(flat_shape).astype(jnp.bfloat16), key_out.reshape(flat_shape).astype(jnp.bfloat16), value_out.reshape(flat_shape).astype(jnp.bfloat16))
    query_grad, key_grad, value_grad = lax.map(backward, (query_blocks, key_blocks, value_blocks, prefix_state, suffix_grad, numer_grad))
    return (layer_out.reshape(TOKENS, D), query_grad.reshape(TOKENS, INNER), key_grad.reshape(TOKENS, INNER), value_grad.reshape(TOKENS, INNER))
```

```python
import functools

import jax
import jax.numpy as jnp
from jax import lax
from jax.experimental import pallas as pl
from jax.experimental.pallas import tpu as pltpu
from jax.sharding import PartitionSpec as P

HEAD_DIM = 128
MESH = pl.DeviceIdType.MESH
PLANE = 4
CHUNKS = 8


def prefix_2(value, axis, combine, identity):
    length, position = (lax.axis_size(axis), lax.axis_index(axis))
    everything = lax.all_gather(value, axis)
    start = jnp.broadcast_to(jnp.asarray(identity, value.dtype), value.shape)

    def hop(k, before):
        reached = k < position
        new = combine(before, everything[k])
        return jnp.where(reached, new, before)

    return lax.fori_loop(0, length, hop, start)


def prefix_3(value, axis, combine, identity):
    length, position = (lax.axis_size(axis), lax.axis_index(axis))
    everything = lax.all_gather(value.astype(jnp.bfloat16), axis)
    start = jnp.broadcast_to(jnp.asarray(identity, value.dtype), value.shape)

    def hop(k, before):
        at = length - 1 - k
        reached = at > position
        new = combine(before, everything[at].astype(value.dtype))
        return jnp.where(reached, new, before)

    return lax.fori_loop(0, length, hop, start)


def lower_mask(length):
    row_ids = lax.broadcasted_iota(jnp.int32, (length, length), 0)
    col_ids = lax.broadcasted_iota(jnp.int32, (length, length), 1)
    return row_ids >= col_ids


def add_states(earlier, latter):
    return earlier + latter


def contract_cols(left_side, right_side):
    return lax.dot_general(
        left_side, right_side, (((1,), (1,)), ((), ())), preferred_element_type=jnp.float32
    )


def contract_rows(left_side, right_side):
    return lax.dot_general(
        left_side, right_side, (((0,), (0,)), ((), ())), preferred_element_type=jnp.float32
    )


def contract_mid(left_side, right_side):
    return jnp.dot(left_side, right_side, preferred_element_type=jnp.float32)


def per_device(queries, key_rows, values, out_weight, out_grad):
    length = queries.shape[0]
    heads_here = queries.shape[1] // HEAD_DIM
    query_heads = queries.reshape(length, heads_here, HEAD_DIM)
    key_heads = key_rows.reshape(length, heads_here, HEAD_DIM)
    value_heads = values.reshape(length, heads_here, HEAD_DIM)
    causal = lower_mask(length)[None]
    local_state = jnp.einsum(
        "shd,she->hde", key_heads, value_heads, preferred_element_type=jnp.float32
    )
    prefix = prefix_2(local_state, "seq", add_states, jnp.zeros_like(local_state))
    prefix_low = prefix.astype(jnp.bfloat16)
    scores = jnp.einsum("thd,shd->hts", query_heads, key_heads, preferred_element_type=jnp.float32)
    weights = jnp.where(causal, scores, 0.0).astype(jnp.bfloat16)
    numerator = jnp.einsum("hts,she->the", weights, value_heads, preferred_element_type=jnp.float32)
    numerator = numerator + jnp.einsum(
        "thd,hde->the", query_heads, prefix_low, preferred_element_type=jnp.float32
    )
    spread = jnp.sqrt(jnp.mean(numerator * numerator, axis=-1, keepdims=True) + 1e-06)
    normed = numerator / spread
    attended = normed.astype(jnp.bfloat16).reshape(length, heads_here * HEAD_DIM)
    full_weight = lax.all_gather(out_weight, "seq", axis=1, tiled=True)
    partial_value = jnp.dot(attended, full_weight, preferred_element_type=jnp.float32)
    layer_out = lax.psum_scatter(
        partial_value.astype(jnp.bfloat16), "head", scatter_dimension=1, tiled=True
    )
    out_dir = contract_cols(lax.all_gather(out_grad, "head", axis=1, tiled=True), full_weight)
    out_dir = out_dir.reshape(length, heads_here, HEAD_DIM)
    along_dir = jnp.mean(out_dir * normed, axis=-1, keepdims=True)
    numer_grad = ((out_dir - normed * along_dir) / spread).astype(jnp.bfloat16)
    local_grad = jnp.einsum(
        "thd,the->hde", query_heads, numer_grad, preferred_element_type=jnp.float32
    )
    suffix = prefix_3(local_grad, "seq", add_states, jnp.zeros_like(local_grad))
    suffix_low = suffix.astype(jnp.bfloat16)
    pair_scores = jnp.einsum(
        "the,she->hts", numer_grad, value_heads, preferred_element_type=jnp.float32
    )
    pair_low = jnp.where(causal, pair_scores, 0.0).astype(jnp.bfloat16)
    query_out = jnp.einsum("hts,shd->thd", pair_low, key_heads, preferred_element_type=jnp.float32)
    query_out = query_out + jnp.einsum(
        "the,hde->thd", numer_grad, prefix_low, preferred_element_type=jnp.float32
    )
    key_out = jnp.einsum("hts,thd->shd", pair_low, query_heads, preferred_element_type=jnp.float32)
    key_out = key_out + jnp.einsum(
        "she,hde->shd", value_heads, suffix_low, preferred_element_type=jnp.float32
    )
    value_out = jnp.einsum("hts,the->she", weights, numer_grad, preferred_element_type=jnp.float32)
    value_out = value_out + jnp.einsum(
        "shd,hde->she", key_heads, suffix_low, preferred_element_type=jnp.float32
    )
    flat_shape = (length, heads_here * HEAD_DIM)
    return (
        layer_out,
        query_out.reshape(flat_shape).astype(jnp.bfloat16),
        key_out.reshape(flat_shape).astype(jnp.bfloat16),
        value_out.reshape(flat_shape).astype(jnp.bfloat16),
    )


def kernel(
    blocks, chunks, q_in, k_in, v_in, w_ref, g_ref,
    mixed_ref, dq_ref, dk_ref, dv_ref,
    q_ref, k_ref, v_ref, w_all, g_all, st_send, st_recv, pre_send, prefix, lg_send, lg_recv, suf_send, suffix,
    out_dir, od_send, od_recv, normed, inv_spread, weights, att, p_own, p_send, p_recv, m_send, m_recv,
    ng, k_part, v_part, x_send, x_recv,
    w_recv_sem, wy_sem, wi_sem, wo_sem, local_sem, g_send_sem, g_recv_sem, a_send_sem, a_recv_sem,
    p_send_sem, p_recv_sem, m_send_sem, m_recv_sem, t_send_sem, t_recv_sem, o_send_sem, o_recv_sem,
    x_send_sem, x_recv_sem,
):
    me = lax.axis_index("seq")
    core = lax.axis_index("head")
    other = 1 - core
    planes = blocks // PLANE
    size = blocks // 2
    share = st_send.shape[0] // size
    team, rank = me // size, lax.rem(me, size)
    spot = lax.rem(me, PLANE)
    level = me // PLANE
    bit_x, bit_y = lax.rem(spot, 2), spot // 2
    length, width = q_ref.shape
    heads = width // HEAD_DIM
    rows, cols = w_ref.shape
    chunk = rows // chunks
    per = chunks // 2
    chunk_heads = chunk // HEAD_DIM
    lower = level < planes // 2
    middle = jnp.where(lower, level, planes - 1 - level) > 0
    edge = jnp.logical_not(middle)
    nbr_x = me + 1 - 2 * bit_x
    nbr_y = me + 2 - 4 * bit_y
    step_in = jnp.where(lower, PLANE, -PLANE)
    inner = me + step_in
    outer = jnp.where(middle, me - step_in, inner)

    def at_seq(position):
        return (position, core)

    def own_col(k):
        return jnp.where(lower, k, planes - 1 - k) * 2 + bit_y

    def other_col(k):
        return jnp.where(lower, k, planes - 1 - k) * 2 + 1 - bit_y

    o0, o1, o2, o3 = (own_col(k) for k in range(4))
    c0, c1, c2, c3 = (other_col(k) for k in range(4))
    mine = me // 2
    near_own = jnp.where(middle, o0, o1)
    near_other, next_other = jnp.where(middle, c1, c0), jnp.where(middle, c0, c1)
    groups = ((mine, near_own, near_other), (o2, next_other), (o3, c2), (c3,))

    q_load = pltpu.make_async_copy(q_in, q_ref, local_sem.at[0])
    k_load = pltpu.make_async_copy(k_in, k_ref, local_sem.at[1])
    v_load = pltpu.make_async_copy(v_in, v_ref, local_sem.at[2])
    own_w = pltpu.make_async_copy(w_ref, w_all.at[mine], local_sem.at[3])
    k_load.start()
    v_load.start()
    barrier = pltpu.get_barrier_semaphore()

    def greet(i, carry):
        pl.semaphore_signal(barrier, inc=1, device_id=at_seq(lax.rem(me + i, blocks)), device_id_type=MESH)
        return carry

    lax.fori_loop(1, blocks, greet, 0)
    pl.semaphore_signal(barrier, inc=1, device_id=(me, other), device_id_type=MESH)

    half = size // 2
    own_rows, far_rows = pl.ds(0, length), pl.ds(length, length)

    def grad_cols(j, parity):
        return pl.ds(pl.multiple_of((lax.rem(j, half) * 2 + parity) * cols, cols), cols)

    def own_grad(i):
        j = core * half + i
        return pltpu.make_async_copy(g_ref.at[:, grad_cols(j, bit_x)], g_all.at[j, own_rows], local_sem.at[4 + i])

    def grad_core(i):
        j = core * half + i
        return pltpu.make_async_remote_copy(
            src_ref=g_ref.at[:, grad_cols(j, bit_x)], dst_ref=g_all.at[j, own_rows],
            send_sem=g_send_sem.at[0, i], recv_sem=g_recv_sem.at[0, i],
            device_id=(me, other), device_id_type=MESH,
        )

    def grad_pair(i):
        j = core * half + i
        return pltpu.make_async_remote_copy(
            src_ref=g_ref.at[:, grad_cols(j, 1 - bit_x)], dst_ref=g_all.at[j, far_rows],
            send_sem=g_send_sem.at[1, i], recv_sem=g_recv_sem.at[1, i],
            device_id=at_seq(nbr_x), device_id_type=MESH,
        )

    def grad_relay(i):
        j = core * half + i
        return pltpu.make_async_remote_copy(
            src_ref=g_all.at[j, far_rows], dst_ref=g_all.at[j, far_rows],
            send_sem=g_send_sem.at[2, i], recv_sem=g_recv_sem.at[2, i],
            device_id=(me, other), device_id_type=MESH,
        )

    q_load.start()
    own_w.start()
    for i in range(half):
        own_grad(i).start()
    k_load.wait()
    v_load.wait()

    def head_cols(h):
        return pl.ds(pl.multiple_of(h * HEAD_DIM, HEAD_DIM), HEAD_DIM)

    def make_state(h, carry):
        c = head_cols(h)
        st_send[h] = contract_rows(k_ref[:, c], v_ref[:, c]).astype(jnp.bfloat16)
        return carry

    lax.fori_loop(0, heads, make_state, 0)
    st_recv[rank] = st_send[pl.ds(rank * share, share)]

    pl.semaphore_wait(barrier, blocks)

    def state_copy(src, dst, kind, peer):
        return pltpu.make_async_remote_copy(
            src_ref=src(peer), dst_ref=dst(rank),
            send_sem=a_send_sem.at[kind, peer], recv_sem=a_recv_sem.at[kind, rank],
            device_id=at_seq(team * size + peer), device_id_type=MESH,
        )

    def leave(src, dst, kind, peer):
        @pl.when(peer != rank)
        def _():
            state_copy(src, dst, kind, peer).start()

    def exchange(src, dst, kind, start):
        def one(i, carry):
            copy = state_copy(src, dst, kind, lax.rem(rank + i, size))
            copy.start() if start else copy.wait_send()
            return carry

        lax.fori_loop(1, size, one, 0)

    def arrived(src, dst, kind):
        def one(i, carry):
            peer = lax.rem(rank + i, size)
            pltpu.make_async_remote_copy(
                src_ref=src(rank), dst_ref=dst(peer),
                send_sem=a_send_sem.at[kind, rank], recv_sem=a_recv_sem.at[kind, peer],
                device_id=at_seq(team * size + peer), device_id_type=MESH,
            ).wait_recv()
            return carry

        lax.fori_loop(1, size, one, 0)

    def pair_of(ref):
        return lambda owner: ref.at[pl.ds(owner * share, share)]

    def slot_of(ref):
        return lambda owner: ref.at[owner]

    def team_total(kind):
        return pltpu.make_async_remote_copy(
            src_ref=x_send.at[kind], dst_ref=x_recv.at[kind],
            send_sem=x_send_sem.at[kind], recv_sem=x_recv_sem.at[kind],
            device_id=at_seq((1 - team) * size + rank), device_id_type=MESH,
        )

    def running(first_team, kind, source, low_send, low_own, backwards):
        @pl.when(team == first_team)
        def _():
            x_recv[kind] = jnp.zeros(x_recv.shape[1:], jnp.float32)

        @pl.when(team != first_team)
        def _():
            team_total(kind).wait_recv()

        def one(i, total):
            at = size - 1 - i if backwards else i
            low_send[at] = total.astype(jnp.bfloat16)
            return total + source[at].astype(jnp.float32)

        x_send[kind] = lax.fori_loop(0, size, one, x_recv[kind])
        low_own[pl.ds(rank * share, share)] = low_send[rank]

        @pl.when(team == first_team)
        def _():
            team_total(kind).start()

    def span_of(c):
        return pl.ds(pl.multiple_of(c * chunk, chunk), chunk)

    def piece(j, c, sems, target, own=False):
        span = span_of(c)
        return pltpu.make_async_remote_copy(
            src_ref=w_ref.at[span] if own else w_all.at[j, span],
            dst_ref=w_all.at[j, span],
            send_sem=sems.at[j, c], recv_sem=w_recv_sem.at[j, c],
            device_id=at_seq(target), device_id_type=MESH,
        )

    def to_y(j, c, own=False):
        return piece(j, c, wy_sem, nbr_y, own)

    def to_inner(j, c, own=False):
        return piece(j, c, wi_sem, inner, own)

    def to_outer(j, c, own=False):
        return piece(j, c, wo_sem, outer, own)

    def landed(j, c):
        to_y(j, c).wait_recv()

    def own_piece(c, finish=False):
        for copy in (to_y(mine, c, True), to_inner(mine, c, True)):
            copy.wait_send() if finish else copy.start()

        @pl.when(middle)
        def _():
            copy = to_outer(mine, c, True)
            copy.wait_send() if finish else copy.start()

    def routed(c):
        return lax.rem(c, 2) == 1

    def pump(phase, c, finish=False):
        def move(j, ways):
            if not finish:
                landed(j, c)
            for way in ways:
                copy = way(j, c)
                copy.wait_send() if finish else copy.start()

        if phase == 0:

            @pl.when(edge)
            def _():
                move(c0, (to_inner,))
                move(o1, (to_y,))

            @pl.when(middle)
            def _():
                move(o0, (to_inner,))
                move(o2, (to_outer, to_y))

        elif phase == 1:

            @pl.when(edge)
            def _():
                move(o2, (to_y,))

            @pl.when(middle)
            def _():
                move(o3, (to_outer, to_y))

        else:

            @pl.when(edge)
            def _():
                if not finish:
                    landed(o3, c)

                @pl.when(jnp.logical_not(routed(c)))
                def _():
                    copy = to_y(o3, c)
                    copy.wait_send() if finish else copy.start()

            @pl.when(middle)
            def _():
                if not finish:
                    landed(c3, c)

                @pl.when(routed(c))
                def _():
                    copy = to_outer(c3, c)
                    copy.wait_send() if finish else copy.start()

    def settle(group, c):
        if group == 0:

            @pl.when(middle)
            def _():
                landed(c1, c)

        elif group == 1:
            landed(next_other, c)
        elif group == 2:
            landed(c2, c)
        else:

            @pl.when(edge)
            def _():
                landed(c3, c)

    causal = lower_mask(length)

    def score_step(h, carry):
        c = head_cols(h)
        kept = jnp.where(causal, contract_cols(q_ref[:, c], k_ref[:, c]), 0.0).astype(jnp.bfloat16)
        weights[h] = kept
        normed[h] = contract_mid(kept, v_ref[:, c])
        return carry

    def norm_step(h, carry):
        c = head_cols(h)
        numerator = normed[h] + contract_mid(q_ref[:, c], prefix[h])
        inv = 1.0 / jnp.sqrt(jnp.mean(numerator * numerator, axis=-1, keepdims=True) + 1e-06)
        value = numerator * inv
        normed[h] = value
        inv_spread[h] = jnp.broadcast_to(inv, (length, HEAD_DIM))
        att[own_rows, c] = value.astype(jnp.bfloat16)
        return carry

    quarter = width // 4

    def att_copy(i):
        c = pl.ds(i * quarter, quarter)
        return pltpu.make_async_remote_copy(
            src_ref=att.at[own_rows, c], dst_ref=att.at[far_rows, c],
            send_sem=t_send_sem.at[i], recv_sem=t_recv_sem.at[i],
            device_id=at_seq(nbr_x), device_id_type=MESH,
        )

    def od_copy(c):
        return pltpu.make_async_remote_copy(
            src_ref=od_send.at[c], dst_ref=od_recv.at[c],
            send_sem=o_send_sem.at[c], recv_sem=o_recv_sem.at[c],
            device_id=at_seq(nbr_x), device_id_type=MESH,
        )

    def direction_step(group, c):
        span = span_of(c)
        total = None
        for j in groups[group]:
            term = contract_cols(g_all[j], w_all[j, span])
            total = term if total is None else total + term
        if group > 0:
            total = total + out_dir[:, span]
        if group < len(groups) - 1:
            out_dir[:, span] = total
        else:
            out_dir[own_rows, span] = total[:length]
            od_send[c] = total[length:].astype(jnp.bfloat16)
            od_copy(c).start()

    def p_copy(slot):
        return pltpu.make_async_remote_copy(
            src_ref=p_send.at[slot], dst_ref=p_recv.at[slot],
            send_sem=p_send_sem.at[slot], recv_sem=p_recv_sem.at[slot],
            device_id=(me, other), device_id_type=MESH,
        )

    def m_copy(slot):
        return pltpu.make_async_remote_copy(
            src_ref=m_send.at[slot], dst_ref=m_recv.at[slot],
            send_sem=m_send_sem.at[slot], recv_sem=m_recv_sem.at[slot],
            device_id=at_seq(nbr_x), device_id_type=MESH,
        )

    def partial_step(j):
        term = contract_mid(att[...], w_all[j]).astype(jnp.bfloat16)
        slot = lax.rem(j, half)

        @pl.when(j // half == core)
        def _():
            p_own[slot] = term

        @pl.when(j // half != core)
        def _():
            p_send[slot] = term
            p_copy(slot).start()

    def mixed_cols(slot, parity):
        return pl.ds(pl.multiple_of((slot * 2 + parity) * cols, cols), cols)

    def mix_step(slot, carry):
        p_copy(slot).wait_recv()
        both = (p_own[slot].astype(jnp.float32) + p_recv[slot].astype(jnp.float32)).astype(jnp.bfloat16)
        m_send[slot] = both[length:]
        m_copy(slot).start()
        mixed_ref[:, mixed_cols(slot, bit_x)] = both[:length]
        return carry

    def numer_step(h, carry):
        c = head_cols(h)
        sub = pl.ds(pl.multiple_of(lax.rem(h, chunk_heads) * HEAD_DIM, HEAD_DIM), HEAD_DIM)
        toward = out_dir[own_rows, c] + od_recv[h // chunk_heads, :, sub].astype(jnp.float32)
        unit = normed[h]
        along = jnp.mean(toward * unit, axis=-1, keepdims=True)
        low = ((toward - unit * along) * inv_spread[h]).astype(jnp.bfloat16)
        ng[:, c] = low
        lg_send[h] = contract_rows(q_ref[:, c], low).astype(jnp.bfloat16)
        return carry

    def numer_chunk(c):
        od_copy(c).wait_recv()
        lax.fori_loop(c * chunk_heads, (c + 1) * chunk_heads, numer_step, 0)
        leave(pair_of(lg_send), slot_of(lg_recv), 2, c)

    def pair_step(h, carry):
        c = head_cols(h)
        low = ng[:, c]
        pair = jnp.where(causal, contract_cols(low, v_ref[:, c]), 0.0).astype(jnp.bfloat16)
        dq_ref[:, c] = (contract_mid(pair, k_ref[:, c]) + contract_cols(low, prefix[h])).astype(jnp.bfloat16)
        k_part[h] = contract_rows(pair, q_ref[:, c])
        v_part[h] = contract_rows(weights[h], low)
        return carry

    def each(count, body):
        def one(i, carry):
            body(i)
            return carry

        lax.fori_loop(0, count, one, 0)

    exchange(pair_of(st_send), slot_of(st_recv), 0, True)
    for i in range(half):
        grad_core(i).start()
        grad_pair(i).start()
    each(per, own_piece)

    q_load.wait()

    def stage(i):
        lax.fori_loop(i * (heads // per), (i + 1) * (heads // per), score_step, 0)
        pump(0, i)

    each(per, stage)
    arrived(pair_of(st_send), slot_of(st_recv), 0)
    running(0, 0, st_recv, pre_send, prefix, False)
    exchange(slot_of(pre_send), pair_of(prefix), 1, True)
    for i in range(half):
        grad_pair(i).wait_recv()
        grad_relay(i).start()
    own_w.wait()
    for i in range(half):
        own_grad(i).wait()
        grad_core(i).wait_recv()
    each(per, lambda i: pump(1, i))
    for i in range(half):
        grad_relay(i).wait_recv()

    def stage(i):
        settle(0, i)
        direction_step(0, i)

    each(per, stage)
    arrived(slot_of(pre_send), pair_of(prefix), 1)

    def stage(i):
        lax.fori_loop(i * (heads // per), (i + 1) * (heads // per), norm_step, 0)
        att_copy(i).start()
        pump(2, i)
        settle(1, i)
        direction_step(1, i)

    for i in range(per):
        stage(i)
    each(per, lambda i: own_piece(per + i))

    def stage(i):
        settle(2, i)
        direction_step(2, i)

    each(per, stage)

    def stage(i):
        settle(3, i)
        direction_step(3, i)

    each(per, stage)

    def stage(i):
        pump(0, per + i)
        numer_chunk(i)

    each(per, stage)
    for i in range(4):
        att_copy(i).wait_recv()

    def stage(i):
        pump(1, per + i)
        settle(0, per + i)
        direction_step(0, per + i)
        lax.fori_loop(i * chunk_heads, (i + 1) * chunk_heads, pair_step, 0)

    each(per, stage)
    for j in groups[0]:
        partial_step(j)

    def stage(i):
        pump(2, per + i)
        settle(1, per + i)
        direction_step(1, per + i)

    each(per, stage)
    for j in groups[1]:
        partial_step(j)

    def stage(i):
        settle(2, per + i)
        direction_step(2, per + i)

    each(per, stage)

    def stage(i):
        settle(3, per + i)
        direction_step(3, per + i)

    each(per, stage)
    for j in groups[2] + groups[3]:
        partial_step(j)
    each(per, lambda i: numer_chunk(per + i))
    lg_recv[rank] = lg_send[pl.ds(rank * share, share)]
    lax.fori_loop(0, half, mix_step, 0)
    arrived(pair_of(lg_send), slot_of(lg_recv), 2)
    running(1, 1, lg_recv, suf_send, suffix, True)
    exchange(slot_of(suf_send), pair_of(suffix), 3, True)
    lax.fori_loop(heads // 2, heads, pair_step, 0)

    def take_mixed(slot, carry):
        m_copy(slot).wait_recv()
        mixed_ref[:, mixed_cols(slot, 1 - bit_x)] = m_recv[slot]
        return carry

    lax.fori_loop(0, half, take_mixed, 0)
    arrived(slot_of(suf_send), pair_of(suffix), 3)

    def last_step(h, carry):
        c = head_cols(h)
        dk_ref[:, c] = (k_part[h] + contract_cols(v_ref[:, c], suffix[h])).astype(jnp.bfloat16)
        dv_ref[:, c] = (v_part[h] + contract_mid(k_ref[:, c], suffix[h])).astype(jnp.bfloat16)
        return carry

    lax.fori_loop(0, heads, last_step, 0)

    def finish(c):
        own_piece(c, True)
        for phase in range(3):
            pump(phase, c, True)
        od_copy(c).wait_send()

    each(chunks, finish)

    def finish(i):
        for copy in (grad_core(i), grad_pair(i), grad_relay(i), p_copy(i), m_copy(i)):
            copy.wait_send()

    each(half, finish)
    for i in range(4):
        att_copy(i).wait_send()
    exchange(pair_of(st_send), slot_of(st_recv), 0, False)
    exchange(slot_of(pre_send), pair_of(prefix), 1, False)
    exchange(pair_of(lg_send), slot_of(lg_recv), 2, False)
    exchange(slot_of(suf_send), pair_of(suffix), 3, False)
    for kind in range(2):

        @pl.when(team == kind)
        def _():
            team_total(kind).wait_send()


def store_kernel(*refs):
    count = (len(refs) - 1) // 2
    copies = [pltpu.make_async_copy(refs[i], refs[count + i], refs[-1].at[i]) for i in range(count)]
    for copy in copies:
        copy.start()
    for copy in copies:
        copy.wait()


def store(*arrays):
    count = len(arrays)
    return pl.pallas_call(
        store_kernel,
        out_shape=tuple(jax.ShapeDtypeStruct(a.shape, a.dtype) for a in arrays),
        in_specs=[pl.BlockSpec(memory_space=pltpu.VMEM)] * count,
        out_specs=(pl.BlockSpec(memory_space=pltpu.HBM),) * count,
        scratch_shapes=[pltpu.SemaphoreType.DMA((count,))],
        compiler_params=pltpu.CompilerParams(vmem_limit_bytes=8 * 2**20),
    )(*arrays)


def fused(blocks, queries, key_rows, values, out_weight, out_grad):
    length, width = queries.shape
    heads = width // HEAD_DIM
    rows, cols = out_weight.shape
    low, wide = jnp.bfloat16, jnp.float32
    size = blocks // 2
    half = size // 2
    share = heads // size
    chunks = CHUNKS
    state = pltpu.VMEM((heads, HEAD_DIM, HEAD_DIM), low)
    slots = pltpu.VMEM((size, share, HEAD_DIM, HEAD_DIM), low)
    totals = pltpu.VMEM((2, share, HEAD_DIM, HEAD_DIM), wide)
    by_head = pltpu.VMEM((heads, length, HEAD_DIM), wide)
    flat = pltpu.VMEM((length, width), low)
    parts = pltpu.VMEM((half, 2 * length, cols), low)
    shares = pltpu.VMEM((half, length, cols), low)
    steps = pltpu.VMEM((chunks, length, rows // chunks), low)
    dma = pltpu.SemaphoreType.DMA
    out = jax.ShapeDtypeStruct((length, width), low)
    vmem, in_hbm = pl.BlockSpec(memory_space=pltpu.VMEM), pl.BlockSpec(memory_space=pltpu.HBM)
    pieces = dma((size, chunks))
    results = pl.pallas_call(
        functools.partial(kernel, blocks, chunks),
        out_shape=(out, out, out, out),
        in_specs=[in_hbm] * 5,
        out_specs=(vmem, vmem, vmem, vmem),
        scratch_shapes=[
            flat, flat, flat,
            pltpu.VMEM((size, rows, cols), low),
            pltpu.VMEM((size, 2 * length, cols), low),
            state, slots, slots, state, state, slots, slots, state,
            pltpu.VMEM((2 * length, rows), wide),
            steps, steps,
            by_head, by_head,
            pltpu.VMEM((heads, length, length), low),
            pltpu.VMEM((2 * length, width), low),
            parts, parts, parts, shares, shares,
            flat, by_head, by_head,
            totals, totals,
            pieces, pieces, pieces, pieces,
            dma((4 + half,)), dma((3, half)), dma((3, half)), dma((4, blocks)), dma((4, blocks)),
            dma((half,)), dma((half,)), dma((half,)), dma((half,)), dma((4,)), dma((4,)),
            dma((chunks,)), dma((chunks,)),
            dma((2,)), dma((2,)),
        ],
        compiler_params=pltpu.CompilerParams(
            collective_id=0, has_side_effects=True, vmem_limit_bytes=44 * 2**20
        ),
    )(queries, key_rows, values, out_weight, out_grad)
    return store(*results)


def solution(mesh):
    blocks, cores = mesh.shape["seq"], mesh.shape["head"]

    def step(queries, key_rows, values, out_weight, out_grad):
        heads = queries.shape[1] // HEAD_DIM
        fits = cores == 2 and blocks == PLANE * PLANE and heads == blocks and out_weight.shape[1] % HEAD_DIM == 0
        fits = fits and out_weight.shape[0] == queries.shape[1] and out_weight.shape[0] % out_weight.shape[1] == 0
        if fits and out_weight.shape[1] * blocks == queries.shape[1] * cores:
            return fused(blocks, queries, key_rows, values, out_weight, out_grad)
        return per_device(queries, key_rows, values, out_weight, out_grad)

    placed = (
        P("seq", "head"),
        P("seq", "head"),
        P("seq", "head"),
        P("head", "seq"),
        P("seq", "head"),
    )
    return jax.shard_map(
        step,
        mesh=mesh,
        in_specs=placed,
        out_specs=(P("seq", "head"), P("seq", "head"), P("seq", "head"), P("seq", "head")),
        check_vma=False,
    )
```

```python
import functools

import jax
import jax.numpy as jnp
from jax import lax
from jax.experimental import pallas as pl
from jax.experimental.pallas import tpu as pltpu
from jax.sharding import PartitionSpec as P

HEAD_DIM = 128
MESH = pl.DeviceIdType.MESH
PLANE = 4
PARTS = (3, 3, 2)
TILE = 64


def prefix_2(value, axis, combine, identity):
    length, position = (lax.axis_size(axis), lax.axis_index(axis))
    everything = lax.all_gather(value, axis)
    start = jnp.broadcast_to(jnp.asarray(identity, value.dtype), value.shape)

    def hop(k, before):
        reached = k < position
        new = combine(before, everything[k])
        return jnp.where(reached, new, before)

    return lax.fori_loop(0, length, hop, start)


def prefix_3(value, axis, combine, identity):
    length, position = (lax.axis_size(axis), lax.axis_index(axis))
    everything = lax.all_gather(value.astype(jnp.bfloat16), axis)
    start = jnp.broadcast_to(jnp.asarray(identity, value.dtype), value.shape)

    def hop(k, before):
        at = length - 1 - k
        reached = at > position
        new = combine(before, everything[at].astype(value.dtype))
        return jnp.where(reached, new, before)

    return lax.fori_loop(0, length, hop, start)


def lower_mask(length):
    row_ids = lax.broadcasted_iota(jnp.int32, (length, length), 0)
    col_ids = lax.broadcasted_iota(jnp.int32, (length, length), 1)
    return row_ids >= col_ids


def add_states(earlier, latter):
    return earlier + latter


def contract_cols(left_side, right_side):
    return lax.dot_general(
        left_side, right_side, (((1,), (1,)), ((), ())), preferred_element_type=jnp.float32
    )


def contract_rows(left_side, right_side):
    return lax.dot_general(
        left_side, right_side, (((0,), (0,)), ((), ())), preferred_element_type=jnp.float32
    )


def contract_mid(left_side, right_side):
    return jnp.dot(left_side, right_side, preferred_element_type=jnp.float32)


def per_device(queries, key_rows, values, out_weight, out_grad):
    length = queries.shape[0]
    heads_here = queries.shape[1] // HEAD_DIM
    query_heads = queries.reshape(length, heads_here, HEAD_DIM)
    key_heads = key_rows.reshape(length, heads_here, HEAD_DIM)
    value_heads = values.reshape(length, heads_here, HEAD_DIM)
    causal = lower_mask(length)[None]
    local_state = jnp.einsum(
        "shd,she->hde", key_heads, value_heads, preferred_element_type=jnp.float32
    )
    prefix = prefix_2(local_state, "seq", add_states, jnp.zeros_like(local_state))
    prefix_low = prefix.astype(jnp.bfloat16)
    scores = jnp.einsum("thd,shd->hts", query_heads, key_heads, preferred_element_type=jnp.float32)
    weights = jnp.where(causal, scores, 0.0).astype(jnp.bfloat16)
    numerator = jnp.einsum("hts,she->the", weights, value_heads, preferred_element_type=jnp.float32)
    numerator = numerator + jnp.einsum(
        "thd,hde->the", query_heads, prefix_low, preferred_element_type=jnp.float32
    )
    spread = jnp.sqrt(jnp.mean(numerator * numerator, axis=-1, keepdims=True) + 1e-06)
    normed = numerator / spread
    attended = normed.astype(jnp.bfloat16).reshape(length, heads_here * HEAD_DIM)
    full_weight = lax.all_gather(out_weight, "seq", axis=1, tiled=True)
    partial_value = jnp.dot(attended, full_weight, preferred_element_type=jnp.float32)
    layer_out = lax.psum_scatter(
        partial_value.astype(jnp.bfloat16), "head", scatter_dimension=1, tiled=True
    )
    out_dir = contract_cols(lax.all_gather(out_grad, "head", axis=1, tiled=True), full_weight)
    out_dir = out_dir.reshape(length, heads_here, HEAD_DIM)
    along_dir = jnp.mean(out_dir * normed, axis=-1, keepdims=True)
    numer_grad = ((out_dir - normed * along_dir) / spread).astype(jnp.bfloat16)
    local_grad = jnp.einsum(
        "thd,the->hde", query_heads, numer_grad, preferred_element_type=jnp.float32
    )
    suffix = prefix_3(local_grad, "seq", add_states, jnp.zeros_like(local_grad))
    suffix_low = suffix.astype(jnp.bfloat16)
    pair_scores = jnp.einsum(
        "the,she->hts", numer_grad, value_heads, preferred_element_type=jnp.float32
    )
    pair_low = jnp.where(causal, pair_scores, 0.0).astype(jnp.bfloat16)
    query_out = jnp.einsum("hts,shd->thd", pair_low, key_heads, preferred_element_type=jnp.float32)
    query_out = query_out + jnp.einsum(
        "the,hde->thd", numer_grad, prefix_low, preferred_element_type=jnp.float32
    )
    key_out = jnp.einsum("hts,thd->shd", pair_low, query_heads, preferred_element_type=jnp.float32)
    key_out = key_out + jnp.einsum(
        "she,hde->shd", value_heads, suffix_low, preferred_element_type=jnp.float32
    )
    value_out = jnp.einsum("hts,the->she", weights, numer_grad, preferred_element_type=jnp.float32)
    value_out = value_out + jnp.einsum(
        "shd,hde->she", key_heads, suffix_low, preferred_element_type=jnp.float32
    )
    flat_shape = (length, heads_here * HEAD_DIM)
    return (
        layer_out,
        query_out.reshape(flat_shape).astype(jnp.bfloat16),
        key_out.reshape(flat_shape).astype(jnp.bfloat16),
        value_out.reshape(flat_shape).astype(jnp.bfloat16),
    )


def kernel(
    blocks, chunks, parts, q_in, k_in, v_in, w_ref, g_ref,
    mixed_ref, dq_ref, dk_ref, dv_ref,
    q_ref, k_ref, v_ref, w_all, g_all, st_send, prefix, lg_send, suffix, a_buf, b_send, b_buf, c_send,
    out_dir, od_send, od_recv, normed, inv_spread, weights, att, p_own, p_send, p_recv, m_send, m_recv,
    ng, k_part, v_part,
    w_recv_sem, wy_sem, wi_sem, wo_sem, local_sem, g_send_sem, g_recv_sem,
    a_send_sem, a_recv_sem, b_send_sem, b_recv_sem, c_send_sem, c_recv_sem,
    p_send_sem, p_recv_sem, m_send_sem, m_recv_sem, t_send_sem, t_recv_sem, o_send_sem, o_recv_sem,
):
    me = lax.axis_index("seq")
    core = lax.axis_index("head")
    other = 1 - core
    planes = blocks // PLANE
    size = blocks // 2
    spot = lax.rem(me, PLANE)
    level = me // PLANE
    bit_x, bit_y = lax.rem(spot, 2), spot // 2
    length, width = q_ref.shape
    heads = width // HEAD_DIM
    rows, cols = w_ref.shape
    chunk = rows // chunks
    chunk_heads = chunk // HEAD_DIM
    lower = level < planes // 2
    middle = jnp.where(lower, level, planes - 1 - level) > 0
    edge = jnp.logical_not(middle)
    nbr_x = me + 1 - 2 * bit_x
    nbr_y = me + 2 - 4 * bit_y
    step_in = jnp.where(lower, PLANE, -PLANE)
    inner = me + step_in
    outer = jnp.where(middle, me - step_in, inner)

    def at_seq(position):
        return (position, core)

    def own_col(k):
        return jnp.where(lower, k, planes - 1 - k) * 2 + bit_y

    def other_col(k):
        return jnp.where(lower, k, planes - 1 - k) * 2 + 1 - bit_y

    o0, o1, o2, o3 = (own_col(k) for k in range(4))
    c0, c1, c2, c3 = (other_col(k) for k in range(4))
    mine = me // 2
    near_own = jnp.where(middle, o0, o1)
    near_other, next_other = jnp.where(middle, c1, c0), jnp.where(middle, c0, c1)
    groups = ((mine, near_own, near_other), (o2, next_other), (o3, c2), (c3,))

    q_load = pltpu.make_async_copy(q_in, q_ref, local_sem.at[0])
    k_load = pltpu.make_async_copy(k_in, k_ref, local_sem.at[1])
    v_load = pltpu.make_async_copy(v_in, v_ref, local_sem.at[2])
    own_w = pltpu.make_async_copy(w_ref, w_all.at[mine], local_sem.at[3])
    k_load.start()
    v_load.start()
    barrier = pltpu.get_barrier_semaphore()

    def greet(i, carry):
        for mate in (level * PLANE + lax.rem(spot + i, PLANE), lax.rem(level + i, planes) * PLANE + spot):
            pl.semaphore_signal(barrier, inc=1, device_id=at_seq(mate), device_id_type=MESH)
        return carry

    lax.fori_loop(1, PLANE, greet, 0)
    pl.semaphore_signal(barrier, inc=1, device_id=(me, other), device_id_type=MESH)

    half = size // 2
    own_rows, far_rows = pl.ds(0, length), pl.ds(length, length)

    def grad_cols(j, parity):
        return pl.ds(pl.multiple_of((lax.rem(j, half) * 2 + parity) * cols, cols), cols)

    def own_grad(i):
        j = core * half + i
        return pltpu.make_async_copy(g_ref.at[:, grad_cols(j, bit_x)], g_all.at[j, own_rows], local_sem.at[4 + i])

    def grad_core(i):
        j = core * half + i
        return pltpu.make_async_remote_copy(
            src_ref=g_ref.at[:, grad_cols(j, bit_x)], dst_ref=g_all.at[j, own_rows],
            send_sem=g_send_sem.at[0, i], recv_sem=g_recv_sem.at[0, i],
            device_id=(me, other), device_id_type=MESH,
        )

    def grad_pair(i):
        j = core * half + i
        return pltpu.make_async_remote_copy(
            src_ref=g_ref.at[:, grad_cols(j, 1 - bit_x)], dst_ref=g_all.at[j, far_rows],
            send_sem=g_send_sem.at[1, i], recv_sem=g_recv_sem.at[1, i],
            device_id=at_seq(nbr_x), device_id_type=MESH,
        )

    def grad_relay(i):
        j = core * half + i
        return pltpu.make_async_remote_copy(
            src_ref=g_all.at[j, far_rows], dst_ref=g_all.at[j, far_rows],
            send_sem=g_send_sem.at[2, i], recv_sem=g_recv_sem.at[2, i],
            device_id=(me, other), device_id_type=MESH,
        )

    q_load.start()
    own_w.start()
    for i in range(half):
        own_grad(i).start()
    def head_cols(h):
        return pl.ds(pl.multiple_of(h * HEAD_DIM, HEAD_DIM), HEAD_DIM)

    def make_state(h, carry):
        c = head_cols(h)
        st_send[c] = contract_rows(k_ref[:, c], v_ref[:, c]).astype(jnp.bfloat16)
        return carry

    def at_of(kind):
        first, count = (0, chunks) if kind == 0 else (sum(parts[: kind - 1]), parts[kind - 1])
        quarter = count * chunk // PLANE
        return first * chunk, first * chunk // PLANE, quarter

    def a_copy(kind, peer, sender):
        base, packed, quarter = at_of(kind)
        source = st_send if kind == 0 else lg_send
        return pltpu.make_async_remote_copy(
            src_ref=source.at[pl.ds(base + peer * quarter, quarter)],
            dst_ref=a_buf.at[min(kind, 1), sender, pl.ds(packed, quarter)],
            send_sem=a_send_sem.at[kind, peer], recv_sem=a_recv_sem.at[kind, sender],
            device_id=at_seq(level * PLANE + peer), device_id_type=MESH,
        )

    def b_copy(kind, plane, sender):
        packed, quarter = at_of(kind)[1:]
        return pltpu.make_async_remote_copy(
            src_ref=b_send.at[min(kind, 1), pl.ds(packed, quarter)],
            dst_ref=b_buf.at[min(kind, 1), sender, pl.ds(packed, quarter)],
            send_sem=b_send_sem.at[kind, plane], recv_sem=b_recv_sem.at[kind, sender],
            device_id=at_seq(plane * PLANE + spot), device_id_type=MESH,
        )

    def c_copy(kind, peer, sender):
        base, packed, quarter = at_of(kind)
        target = prefix if kind == 0 else suffix
        return pltpu.make_async_remote_copy(
            src_ref=c_send.at[min(kind, 1), peer, pl.ds(packed, quarter)],
            dst_ref=target.at[pl.ds(base + sender * quarter, quarter)],
            send_sem=c_send_sem.at[kind, peer], recv_sem=c_recv_sem.at[kind, sender],
            device_id=at_seq(level * PLANE + peer), device_id_type=MESH,
        )

    def mates(body):
        def one(i, carry):
            body(lax.rem(spot + i, PLANE))
            return carry

        lax.fori_loop(1, PLANE, one, 0)

    def later(kind, body):
        def one(i, carry):
            plane = level + i if kind == 0 else level - i

            @pl.when(jnp.logical_and(plane >= 0, plane < planes))
            def _():
                body(jnp.clip(plane, 0, planes - 1))

            return carry

        lax.fori_loop(1, planes, one, 0)

    def earlier(kind, body):
        later(1 - min(kind, 1), body)

    def tiles(kind, body):
        packed, quarter = at_of(kind)[1:]

        def one(i, carry):
            body(pl.multiple_of(i * TILE, TILE), pl.ds(pl.multiple_of(packed + i * TILE, TILE), TILE))
            return carry

        lax.fori_loop(0, quarter // TILE, one, 0)

    def own_quarter(kind):
        base, packed, quarter = at_of(kind)
        source = st_send if kind == 0 else lg_send
        a_buf[min(kind, 1), spot, pl.ds(packed, quarter)] = source[pl.ds(base + spot * quarter, quarter)]

    def scan_open(kind):
        mates(lambda peer: a_copy(kind, peer, spot).start())
        own_quarter(kind)

    def scan_planes(kind):
        way = min(kind, 1)
        mates(lambda peer: a_copy(kind, spot, peer).wait_recv())

        def tile(_, here):
            total = a_buf[way, 0, here].astype(jnp.float32)
            for s in range(1, PLANE):
                total = total + a_buf[way, s, here].astype(jnp.float32)
            b_send[way, here] = total.astype(jnp.bfloat16)

        tiles(kind, tile)
        later(kind, lambda plane: b_copy(kind, plane, level).start())

    def scan_close(kind):
        base, packed, quarter = at_of(kind)
        way = min(kind, 1)
        target = prefix if kind == 0 else suffix
        earlier(kind, lambda plane: b_copy(kind, level, plane).wait_recv())

        def tile(_, here):
            total = b_buf[way, 0, here].astype(jnp.float32)
            for z in range(1, planes):
                total = total + b_buf[way, z, here].astype(jnp.float32)
            for s in range(PLANE) if kind == 0 else range(PLANE - 1, -1, -1):
                c_send[way, s, here] = total.astype(jnp.bfloat16)
                total = total + a_buf[way, s, here].astype(jnp.float32)

        tiles(kind, tile)
        mates(lambda peer: c_copy(kind, peer, spot).start())
        target[pl.ds(base + spot * quarter, quarter)] = c_send[way, spot, pl.ds(packed, quarter)]

    def scan_end(kind):
        mates(lambda peer: c_copy(kind, spot, peer).wait_recv())

    def scan_sent(kind):
        mates(lambda peer: a_copy(kind, peer, spot).wait_send())
        later(kind, lambda plane: b_copy(kind, plane, level).wait_send())
        mates(lambda peer: c_copy(kind, peer, spot).wait_send())

    def span_of(c):
        return pl.ds(pl.multiple_of(c * chunk, chunk), chunk)

    def piece(j, c, sems, target, own=False):
        span = span_of(c)
        return pltpu.make_async_remote_copy(
            src_ref=w_ref.at[span] if own else w_all.at[j, span],
            dst_ref=w_all.at[j, span],
            send_sem=sems.at[j, c], recv_sem=w_recv_sem.at[j, c],
            device_id=at_seq(target), device_id_type=MESH,
        )

    def to_y(j, c, own=False):
        return piece(j, c, wy_sem, nbr_y, own)

    def to_inner(j, c, own=False):
        return piece(j, c, wi_sem, inner, own)

    def to_outer(j, c, own=False):
        return piece(j, c, wo_sem, outer, own)

    def landed(j, c):
        to_y(j, c).wait_recv()

    def own_piece(c, finish=False):
        for copy in (to_y(mine, c, True), to_inner(mine, c, True)):
            copy.wait_send() if finish else copy.start()

        @pl.when(middle)
        def _():
            copy = to_outer(mine, c, True)
            copy.wait_send() if finish else copy.start()

    def routed(c):
        return lax.rem(c, 3) != 0

    def pump(phase, c, finish=False):
        def move(j, ways):
            if not finish:
                landed(j, c)
            for way in ways:
                copy = way(j, c)
                copy.wait_send() if finish else copy.start()

        if phase == 0:

            @pl.when(edge)
            def _():
                move(c0, (to_inner,))
                move(o1, (to_y,))

            @pl.when(middle)
            def _():
                move(o0, (to_inner,))
                move(o2, (to_outer, to_y))

        elif phase == 1:

            @pl.when(edge)
            def _():
                move(o2, (to_y,))

            @pl.when(middle)
            def _():
                move(o3, (to_outer, to_y))

        else:

            @pl.when(edge)
            def _():
                if not finish:
                    landed(o3, c)

                @pl.when(jnp.logical_not(routed(c)))
                def _():
                    copy = to_y(o3, c)
                    copy.wait_send() if finish else copy.start()

            @pl.when(middle)
            def _():
                if not finish:
                    landed(c3, c)

                @pl.when(routed(c))
                def _():
                    copy = to_outer(c3, c)
                    copy.wait_send() if finish else copy.start()

    def settle(group, c):
        if group == 0:

            @pl.when(middle)
            def _():
                landed(c1, c)

        elif group == 1:
            landed(next_other, c)
        elif group == 2:
            landed(c2, c)
        else:

            @pl.when(edge)
            def _():
                landed(c3, c)

    causal = lower_mask(length)

    def score_step(h, carry):
        c = head_cols(h)
        kept = jnp.where(causal, contract_cols(q_ref[:, c], k_ref[:, c]), 0.0).astype(jnp.bfloat16)
        weights[h] = kept
        normed[h] = contract_mid(kept, v_ref[:, c])
        return carry

    def norm_step(h, carry):
        c = head_cols(h)
        numerator = normed[h] + contract_mid(q_ref[:, c], prefix[c])
        inv = 1.0 / jnp.sqrt(jnp.mean(numerator * numerator, axis=-1, keepdims=True) + 1e-06)
        value = numerator * inv
        normed[h] = value
        inv_spread[h] = jnp.broadcast_to(inv, (length, HEAD_DIM))
        att[own_rows, c] = value.astype(jnp.bfloat16)
        return carry

    def att_copy(i):
        c = span_of(i)
        return pltpu.make_async_remote_copy(
            src_ref=att.at[own_rows, c], dst_ref=att.at[far_rows, c],
            send_sem=t_send_sem.at[i], recv_sem=t_recv_sem.at[i],
            device_id=at_seq(nbr_x), device_id_type=MESH,
        )

    def od_copy(c):
        return pltpu.make_async_remote_copy(
            src_ref=od_send.at[c], dst_ref=od_recv.at[c],
            send_sem=o_send_sem.at[c], recv_sem=o_recv_sem.at[c],
            device_id=at_seq(nbr_x), device_id_type=MESH,
        )

    def direction_step(group, c):
        span = span_of(c)
        total = None
        for j in groups[group]:
            term = contract_cols(g_all[j], w_all[j, span])
            total = term if total is None else total + term
        if group > 0:
            total = total + out_dir[:, span]
        if group < len(groups) - 1:
            out_dir[:, span] = total
        else:
            out_dir[own_rows, span] = total[:length]
            od_send[c] = total[length:].astype(jnp.bfloat16)
            od_copy(c).start()

    def p_copy(slot):
        return pltpu.make_async_remote_copy(
            src_ref=p_send.at[slot], dst_ref=p_recv.at[slot],
            send_sem=p_send_sem.at[slot], recv_sem=p_recv_sem.at[slot],
            device_id=(me, other), device_id_type=MESH,
        )

    def m_copy(slot):
        return pltpu.make_async_remote_copy(
            src_ref=m_send.at[slot], dst_ref=m_recv.at[slot],
            send_sem=m_send_sem.at[slot], recv_sem=m_recv_sem.at[slot],
            device_id=at_seq(nbr_x), device_id_type=MESH,
        )

    def partial_step(j):
        term = contract_mid(att[...], w_all[j]).astype(jnp.bfloat16)
        slot = lax.rem(j, half)

        @pl.when(j // half == core)
        def _():
            p_own[slot] = term

        @pl.when(j // half != core)
        def _():
            p_send[slot] = term
            p_copy(slot).start()

    def mixed_cols(slot, parity):
        return pl.ds(pl.multiple_of((slot * 2 + parity) * cols, cols), cols)

    def mix_step(slot, carry):
        p_copy(slot).wait_recv()
        both = (p_own[slot].astype(jnp.float32) + p_recv[slot].astype(jnp.float32)).astype(jnp.bfloat16)
        m_send[slot] = both[length:]
        m_copy(slot).start()
        mixed_ref[:, mixed_cols(slot, bit_x)] = both[:length]
        return carry

    def numer_step(h, carry):
        c = head_cols(h)
        sub = pl.ds(pl.multiple_of(lax.rem(h, chunk_heads) * HEAD_DIM, HEAD_DIM), HEAD_DIM)
        toward = out_dir[own_rows, c] + od_recv[h // chunk_heads, :, sub].astype(jnp.float32)
        unit = normed[h]
        along = jnp.mean(toward * unit, axis=-1, keepdims=True)
        low = ((toward - unit * along) * inv_spread[h]).astype(jnp.bfloat16)
        ng[:, c] = low
        lg_send[c] = contract_rows(q_ref[:, c], low).astype(jnp.bfloat16)
        return carry

    def numer_chunk(c):
        od_copy(c).wait_recv()
        lax.fori_loop(c * chunk_heads, (c + 1) * chunk_heads, numer_step, 0)

    def pair_step(h, carry):
        c = head_cols(h)
        low = ng[:, c]
        pair = jnp.where(causal, contract_cols(low, v_ref[:, c]), 0.0).astype(jnp.bfloat16)
        dq_ref[:, c] = (contract_mid(pair, k_ref[:, c]) + contract_cols(low, prefix[c])).astype(jnp.bfloat16)
        k_part[h] = contract_rows(pair, q_ref[:, c])
        v_part[h] = contract_rows(weights[h], low)
        return carry

    def each(count, body):
        def one(i, carry):
            body(i)
            return carry

        lax.fori_loop(0, count, one, 0)

    def heads_of(c, body):
        lax.fori_loop(c * chunk_heads, (c + 1) * chunk_heads, body, 0)

    def last_step(h, carry):
        c = head_cols(h)
        dk_ref[:, c] = (k_part[h] + contract_cols(v_ref[:, c], suffix[c])).astype(jnp.bfloat16)
        dv_ref[:, c] = (v_part[h] + contract_mid(k_ref[:, c], suffix[c])).astype(jnp.bfloat16)
        return carry

    def each(first, last, body):
        def one(i, carry):
            body(i)
            return carry

        lax.fori_loop(first, last, one, 0)

    def aim(group, first, last):
        def one(c):
            settle(group, c)
            direction_step(group, c)

        each(first, last, one)

    e1, e2, e3 = parts[0], parts[0] + parts[1], chunks

    pl.semaphore_wait(barrier, 2 * PLANE - 1)
    own_piece(0)
    for i in range(half):
        grad_core(i).start()
    each(0, half // 2, lambda i: grad_pair(i).start())
    for z in range(planes):

        @pl.when(z >= level)
        def _():
            b_buf[0, z] = jnp.zeros(b_buf.shape[2:], b_buf.dtype)

        @pl.when(z <= level)
        def _():
            b_buf[1, z] = jnp.zeros(b_buf.shape[2:], b_buf.dtype)

    k_load.wait()
    v_load.wait()
    team = heads // PLANE

    def some_states(peer):
        lax.fori_loop(peer * team, (peer + 1) * team, make_state, 0)

    def open_states(peer):
        some_states(peer)
        a_copy(0, peer, spot).start()

    mates(open_states)
    each(half // 2, half, lambda i: grad_pair(i).start())
    each(1, e1, own_piece)
    some_states(spot)
    own_quarter(0)
    q_load.wait()
    lax.fori_loop(0, heads, score_step, 0)
    scan_planes(0)
    each(0, 2, lambda c: pump(0, c))
    scan_close(0)
    each(2, e1, lambda c: pump(0, c))
    each(0, e1, lambda c: pump(1, c))
    for i in range(half):
        grad_pair(i).wait_recv()
        grad_relay(i).start()
    own_w.wait()
    for i in range(half):
        own_grad(i).wait()
        grad_core(i).wait_recv()
    scan_end(0)

    def stage(c):
        heads_of(c, norm_step)
        att_copy(c).start()

    each(0, 4, stage)
    each(0, e1, lambda c: pump(2, c))
    each(e1, e2, own_piece)
    for i in range(half):
        grad_relay(i).wait_recv()
    each(4, chunks, lambda c: heads_of(c, norm_step))
    aim(0, 0, e1)
    aim(1, 0, e1)
    aim(2, 0, e1)
    aim(3, 0, e1)

    def stage(c):
        pump(0, c)
        att_copy(c - e1 + 4).start()

    each(e1, e2, stage)
    each(e2, e3, own_piece)
    each(e2 - e1 + 4, chunks, lambda c: att_copy(c).start())
    each(0, e1, numer_chunk)
    scan_open(1)
    each(e2, e3, lambda c: pump(0, c))

    def stage(c):
        pump(1, c)
        settle(0, c)
        direction_step(0, c)
        heads_of(c - e1, pair_step)

    each(e1, e2, stage)
    scan_planes(1)

    def stage(c):
        pump(2, c)
        settle(1, c)
        direction_step(1, c)

    each(e1, e2, stage)
    scan_close(1)
    aim(2, e1, e2)
    aim(3, e1, e2)
    each(e2, e3, lambda c: pump(1, c))
    each(0, chunks, lambda c: att_copy(c).wait_recv())
    aim(0, e2, e3)
    aim(1, e2, e3)
    for j in groups[0] + (next_other,):
        partial_step(j)
    each(e2, e3, lambda c: pump(2, c))
    each(e1, e2, numer_chunk)
    scan_open(2)
    near = level // (planes // 2)

    @pl.when(core == near)
    def _():
        lax.fori_loop(0, half, mix_step, 0)

    aim(2, e2, e3)
    scan_planes(2)
    aim(3, e2, e3)
    scan_close(2)
    for j in (o2, o3, c2, c3):
        partial_step(j)
    each(e2, e3, numer_chunk)
    scan_open(3)
    each(e1, e2, lambda c: heads_of(c, pair_step))
    scan_planes(3)

    @pl.when(core != near)
    def _():
        lax.fori_loop(0, half, mix_step, 0)

    each(e2, e3, lambda c: heads_of(c, pair_step))
    scan_end(1)
    scan_close(3)
    each(0, e1, lambda c: heads_of(c, last_step))
    scan_end(2)
    each(e1, e2, lambda c: heads_of(c, last_step))
    scan_end(3)
    each(e2, e3, lambda c: heads_of(c, last_step))

    def take_mixed(slot, carry):
        m_copy(slot).wait_recv()
        mixed_ref[:, mixed_cols(slot, 1 - bit_x)] = m_recv[slot]
        return carry

    lax.fori_loop(0, half, take_mixed, 0)

    def finish(c):
        own_piece(c, True)
        for phase in range(3):
            pump(phase, c, True)
        od_copy(c).wait_send()
        att_copy(c).wait_send()

    each(0, chunks, finish)

    def finish(i):
        for copy in (grad_core(i), grad_pair(i), grad_relay(i), p_copy(i), m_copy(i)):
            copy.wait_send()

    each(0, half, finish)
    for kind in range(len(parts) + 1):
        scan_sent(kind)


def store_kernel(*refs):
    count = (len(refs) - 1) // 2
    copies = [pltpu.make_async_copy(refs[i], refs[count + i], refs[-1].at[i]) for i in range(count)]
    for copy in copies:
        copy.start()
    for copy in copies:
        copy.wait()


def store(*arrays):
    count = len(arrays)
    return pl.pallas_call(
        store_kernel,
        out_shape=tuple(jax.ShapeDtypeStruct(a.shape, a.dtype) for a in arrays),
        in_specs=[pl.BlockSpec(memory_space=pltpu.VMEM)] * count,
        out_specs=(pl.BlockSpec(memory_space=pltpu.HBM),) * count,
        scratch_shapes=[pltpu.SemaphoreType.DMA((count,))],
        compiler_params=pltpu.CompilerParams(vmem_limit_bytes=8 * 2**20),
    )(*arrays)


def fused(blocks, queries, key_rows, values, out_weight, out_grad):
    length, width = queries.shape
    heads = width // HEAD_DIM
    rows, cols = out_weight.shape
    low, wide = jnp.bfloat16, jnp.float32
    size = blocks // 2
    half = size // 2
    chunks = sum(PARTS)
    state = pltpu.VMEM((rows, HEAD_DIM), low)
    fourth = rows // PLANE
    by_spot = pltpu.VMEM((2, PLANE, fourth, HEAD_DIM), low)
    by_head = pltpu.VMEM((heads, length, HEAD_DIM), wide)
    flat = pltpu.VMEM((length, width), low)
    parts = pltpu.VMEM((half, 2 * length, cols), low)
    shares = pltpu.VMEM((half, length, cols), low)
    steps = pltpu.VMEM((chunks, length, rows // chunks), low)
    dma = pltpu.SemaphoreType.DMA
    out = jax.ShapeDtypeStruct((length, width), low)
    vmem, in_hbm = pl.BlockSpec(memory_space=pltpu.VMEM), pl.BlockSpec(memory_space=pltpu.HBM)
    pieces = dma((size, chunks))
    scans = dma((len(PARTS) + 1, PLANE))
    results = pl.pallas_call(
        functools.partial(kernel, blocks, chunks, PARTS),
        out_shape=(out, out, out, out),
        in_specs=[in_hbm] * 5,
        out_specs=(vmem, vmem, vmem, vmem),
        scratch_shapes=[
            flat, flat, flat,
            pltpu.VMEM((size, rows, cols), low),
            pltpu.VMEM((size, 2 * length, cols), low),
            state, state, state, state,
            by_spot, pltpu.VMEM((2, fourth, HEAD_DIM), low), by_spot, by_spot,
            pltpu.VMEM((2 * length, rows), wide),
            steps, steps,
            by_head, by_head,
            pltpu.VMEM((heads, length, length), low),
            pltpu.VMEM((2 * length, width), low),
            parts, parts, parts, shares, shares,
            flat, by_head, by_head,
            pieces, pieces, pieces, pieces,
            dma((4 + half,)), dma((3, half)), dma((3, half)),
            scans, scans, scans, scans, scans, scans,
            dma((half,)), dma((half,)), dma((half,)), dma((half,)), dma((chunks,)), dma((chunks,)),
            dma((chunks,)), dma((chunks,)),
        ],
        compiler_params=pltpu.CompilerParams(
            collective_id=0, has_side_effects=True, vmem_limit_bytes=49 * 2**20
        ),
    )(queries, key_rows, values, out_weight, out_grad)
    return store(*results)


def solution(mesh):
    blocks, cores = mesh.shape["seq"], mesh.shape["head"]

    def step(queries, key_rows, values, out_weight, out_grad):
        heads = queries.shape[1] // HEAD_DIM
        fits = cores == 2 and blocks == PLANE * PLANE and heads == blocks and out_weight.shape[1] % HEAD_DIM == 0
        fits = fits and out_weight.shape[0] == queries.shape[1] and out_weight.shape[0] % out_weight.shape[1] == 0
        if fits and out_weight.shape[1] * blocks == queries.shape[1] * cores:
            return fused(blocks, queries, key_rows, values, out_weight, out_grad)
        return per_device(queries, key_rows, values, out_weight, out_grad)

    placed = (
        P("seq", "head"),
        P("seq", "head"),
        P("seq", "head"),
        P("head", "seq"),
        P("seq", "head"),
    )
    return jax.shard_map(
        step,
        mesh=mesh,
        in_specs=placed,
        out_specs=(P("seq", "head"), P("seq", "head"), P("seq", "head"), P("seq", "head")),
        check_vma=False,
    )
```

```python
import functools

import jax
import jax.numpy as jnp
from jax import lax
from jax.experimental import pallas as pl
from jax.experimental.pallas import tpu as pltpu
from jax.sharding import PartitionSpec as P

HEAD_DIM = 128
MESH = pl.DeviceIdType.MESH
PLANE = 4
PARTS = (3, 3, 2)
TILE = 64


def prefix_2(value, axis, combine, identity):
    length, position = (lax.axis_size(axis), lax.axis_index(axis))
    everything = lax.all_gather(value, axis)
    start = jnp.broadcast_to(jnp.asarray(identity, value.dtype), value.shape)

    def hop(k, before):
        reached = k < position
        new = combine(before, everything[k])
        return jnp.where(reached, new, before)

    return lax.fori_loop(0, length, hop, start)


def prefix_3(value, axis, combine, identity):
    length, position = (lax.axis_size(axis), lax.axis_index(axis))
    everything = lax.all_gather(value.astype(jnp.bfloat16), axis)
    start = jnp.broadcast_to(jnp.asarray(identity, value.dtype), value.shape)

    def hop(k, before):
        at = length - 1 - k
        reached = at > position
        new = combine(before, everything[at].astype(value.dtype))
        return jnp.where(reached, new, before)

    return lax.fori_loop(0, length, hop, start)


def lower_mask(length):
    row_ids = lax.broadcasted_iota(jnp.int32, (length, length), 0)
    col_ids = lax.broadcasted_iota(jnp.int32, (length, length), 1)
    return row_ids >= col_ids


def add_states(earlier, latter):
    return earlier + latter


def contract_cols(left_side, right_side):
    return lax.dot_general(
        left_side, right_side, (((1,), (1,)), ((), ())), preferred_element_type=jnp.float32
    )


def contract_rows(left_side, right_side):
    return lax.dot_general(
        left_side, right_side, (((0,), (0,)), ((), ())), preferred_element_type=jnp.float32
    )


def contract_mid(left_side, right_side):
    return jnp.dot(left_side, right_side, preferred_element_type=jnp.float32)


def per_device(queries, key_rows, values, out_weight, out_grad):
    length = queries.shape[0]
    heads_here = queries.shape[1] // HEAD_DIM
    query_heads = queries.reshape(length, heads_here, HEAD_DIM)
    key_heads = key_rows.reshape(length, heads_here, HEAD_DIM)
    value_heads = values.reshape(length, heads_here, HEAD_DIM)
    causal = lower_mask(length)[None]
    local_state = jnp.einsum(
        "shd,she->hde", key_heads, value_heads, preferred_element_type=jnp.float32
    )
    prefix = prefix_2(local_state, "seq", add_states, jnp.zeros_like(local_state))
    prefix_low = prefix.astype(jnp.bfloat16)
    scores = jnp.einsum("thd,shd->hts", query_heads, key_heads, preferred_element_type=jnp.float32)
    weights = jnp.where(causal, scores, 0.0).astype(jnp.bfloat16)
    numerator = jnp.einsum("hts,she->the", weights, value_heads, preferred_element_type=jnp.float32)
    numerator = numerator + jnp.einsum(
        "thd,hde->the", query_heads, prefix_low, preferred_element_type=jnp.float32
    )
    spread = jnp.sqrt(jnp.mean(numerator * numerator, axis=-1, keepdims=True) + 1e-06)
    normed = numerator / spread
    attended = normed.astype(jnp.bfloat16).reshape(length, heads_here * HEAD_DIM)
    full_weight = lax.all_gather(out_weight, "seq", axis=1, tiled=True)
    partial_value = jnp.dot(attended, full_weight, preferred_element_type=jnp.float32)
    layer_out = lax.psum_scatter(
        partial_value.astype(jnp.bfloat16), "head", scatter_dimension=1, tiled=True
    )
    out_dir = contract_cols(lax.all_gather(out_grad, "head", axis=1, tiled=True), full_weight)
    out_dir = out_dir.reshape(length, heads_here, HEAD_DIM)
    along_dir = jnp.mean(out_dir * normed, axis=-1, keepdims=True)
    numer_grad = ((out_dir - normed * along_dir) / spread).astype(jnp.bfloat16)
    local_grad = jnp.einsum(
        "thd,the->hde", query_heads, numer_grad, preferred_element_type=jnp.float32
    )
    suffix = prefix_3(local_grad, "seq", add_states, jnp.zeros_like(local_grad))
    suffix_low = suffix.astype(jnp.bfloat16)
    pair_scores = jnp.einsum(
        "the,she->hts", numer_grad, value_heads, preferred_element_type=jnp.float32
    )
    pair_low = jnp.where(causal, pair_scores, 0.0).astype(jnp.bfloat16)
    query_out = jnp.einsum("hts,shd->thd", pair_low, key_heads, preferred_element_type=jnp.float32)
    query_out = query_out + jnp.einsum(
        "the,hde->thd", numer_grad, prefix_low, preferred_element_type=jnp.float32
    )
    key_out = jnp.einsum("hts,thd->shd", pair_low, query_heads, preferred_element_type=jnp.float32)
    key_out = key_out + jnp.einsum(
        "she,hde->shd", value_heads, suffix_low, preferred_element_type=jnp.float32
    )
    value_out = jnp.einsum("hts,the->she", weights, numer_grad, preferred_element_type=jnp.float32)
    value_out = value_out + jnp.einsum(
        "shd,hde->she", key_heads, suffix_low, preferred_element_type=jnp.float32
    )
    flat_shape = (length, heads_here * HEAD_DIM)
    return (
        layer_out,
        query_out.reshape(flat_shape).astype(jnp.bfloat16),
        key_out.reshape(flat_shape).astype(jnp.bfloat16),
        value_out.reshape(flat_shape).astype(jnp.bfloat16),
    )


def kernel(
    blocks, chunks, parts, q_in, k_in, v_in, w_ref, g_ref,
    mixed_ref, dq_ref, dk_ref, dv_ref,
    q_ref, k_ref, v_ref, w_all, g_all, st_send, prefix, lg_send, suffix, a_buf, b_send, b_buf, c_send,
    out_dir, od_send, od_recv, normed, inv_spread, weights, att, p_own, p_send, p_recv, m_send, m_recv,
    ng, k_part, v_part,
    w_recv_sem, w_send_sem, local_sem, g_send_sem, g_recv_sem,
    a_send_sem, a_recv_sem, b_send_sem, b_recv_sem, c_send_sem, c_recv_sem,
    p_send_sem, p_recv_sem, m_sem, t_sem, o_send_sem, o_recv_sem,
):
    me = lax.axis_index("seq")
    core = lax.axis_index("head")
    other = 1 - core
    planes = blocks // PLANE
    size = blocks // 2
    spot = lax.rem(me, PLANE)
    level = me // PLANE
    bit_x, bit_y = lax.rem(spot, 2), spot // 2
    length, width = q_ref.shape
    heads = width // HEAD_DIM
    rows, cols = w_ref.shape
    chunk = rows // chunks
    chunk_heads = chunk // HEAD_DIM
    lower = level < planes // 2
    middle = jnp.where(lower, level, planes - 1 - level) > 0
    edge = jnp.logical_not(middle)
    nbr_x = me + 1 - 2 * bit_x
    nbr_y = me + 2 - 4 * bit_y
    step_in = jnp.where(lower, PLANE, -PLANE)
    inner = me + step_in
    outer = jnp.where(middle, me - step_in, inner)

    def at_seq(position):
        return (position, core)

    def own_col(k):
        return jnp.where(lower, k, planes - 1 - k) * 2 + bit_y

    def other_col(k):
        return jnp.where(lower, k, planes - 1 - k) * 2 + 1 - bit_y

    o0, o1, o2, o3 = (own_col(k) for k in range(4))
    c0, c1, c2, c3 = (other_col(k) for k in range(4))
    mine = me // 2
    near_own = jnp.where(middle, o0, o1)
    near_other, next_other = jnp.where(middle, c1, c0), jnp.where(middle, c0, c1)
    groups = ((mine, near_own, near_other), (o2, next_other), (o3, c2), (c3,))

    q_load = pltpu.make_async_copy(q_in, q_ref, local_sem.at[0])
    k_load = pltpu.make_async_copy(k_in, k_ref, local_sem.at[1])
    v_load = pltpu.make_async_copy(v_in, v_ref, local_sem.at[2])
    own_w = pltpu.make_async_copy(w_ref, w_all.at[mine], local_sem.at[3])
    k_load.start()
    v_load.start()
    barrier = pltpu.get_barrier_semaphore()

    def greet(i, carry):
        for mate in (level * PLANE + lax.rem(spot + i, PLANE), lax.rem(level + i, planes) * PLANE + spot):
            pl.semaphore_signal(barrier, inc=1, device_id=at_seq(mate), device_id_type=MESH)
        return carry

    lax.fori_loop(1, PLANE, greet, 0)
    pl.semaphore_signal(barrier, inc=1, device_id=(me, other), device_id_type=MESH)

    half = size // 2
    own_rows, far_rows = pl.ds(0, length), pl.ds(length, length)

    def bulk(ref, sent=None, got=None):
        copy = pltpu.make_async_remote_copy(
            src_ref=ref, dst_ref=ref,
            send_sem=got if sent is None else sent, recv_sem=sent if got is None else got,
            device_id=(me, other), device_id_type=MESH,
        )
        copy.wait_recv() if sent is None else copy.wait_send()

    def grad_cols(j, parity):
        return pl.ds(pl.multiple_of((lax.rem(j, half) * 2 + parity) * cols, cols), cols)

    def own_grad(i):
        j = core * half + i
        return pltpu.make_async_copy(g_ref.at[:, grad_cols(j, bit_x)], g_all.at[j, own_rows], local_sem.at[4])

    def grad_core(i):
        j = core * half + i
        return pltpu.make_async_remote_copy(
            src_ref=g_ref.at[:, grad_cols(j, bit_x)], dst_ref=g_all.at[j, own_rows],
            send_sem=g_send_sem.at[0], recv_sem=g_recv_sem.at[0],
            device_id=(me, other), device_id_type=MESH,
        )

    def grad_pair(i):
        j = core * half + i
        return pltpu.make_async_remote_copy(
            src_ref=g_ref.at[:, grad_cols(j, 1 - bit_x)], dst_ref=g_all.at[j, far_rows],
            send_sem=g_send_sem.at[1], recv_sem=g_recv_sem.at[1],
            device_id=at_seq(nbr_x), device_id_type=MESH,
        )

    def grad_relay(i):
        j = core * half + i
        return pltpu.make_async_remote_copy(
            src_ref=g_all.at[j, far_rows], dst_ref=g_all.at[j, far_rows],
            send_sem=g_send_sem.at[2], recv_sem=g_recv_sem.at[2],
            device_id=(me, other), device_id_type=MESH,
        )

    q_load.start()
    own_w.start()
    for i in range(half):
        own_grad(i).start()
    def head_cols(h):
        return pl.ds(pl.multiple_of(h * HEAD_DIM, HEAD_DIM), HEAD_DIM)

    def make_state(h, carry):
        c = head_cols(h)
        st_send[c] = contract_rows(k_ref[:, c], v_ref[:, c]).astype(jnp.bfloat16)
        return carry

    def at_of(kind):
        first, count = (0, chunks) if kind == 0 else (sum(parts[: kind - 1]), parts[kind - 1])
        quarter = count * chunk // PLANE
        return first * chunk, first * chunk // PLANE, quarter

    def a_copy(kind, peer, sender):
        base, packed, quarter = at_of(kind)
        source = st_send if kind == 0 else lg_send
        return pltpu.make_async_remote_copy(
            src_ref=source.at[pl.ds(base + peer * quarter, quarter)],
            dst_ref=a_buf.at[min(kind, 1), sender, pl.ds(packed, quarter)],
            send_sem=a_send_sem.at[kind], recv_sem=a_recv_sem.at[kind],
            device_id=at_seq(level * PLANE + peer), device_id_type=MESH,
        )

    def b_copy(kind, plane, sender):
        packed, quarter = at_of(kind)[1:]
        return pltpu.make_async_remote_copy(
            src_ref=b_send.at[min(kind, 1), pl.ds(packed, quarter)],
            dst_ref=b_buf.at[min(kind, 1), sender, pl.ds(packed, quarter)],
            send_sem=b_send_sem.at[kind], recv_sem=b_recv_sem.at[kind],
            device_id=at_seq(plane * PLANE + spot), device_id_type=MESH,
        )

    def c_copy(kind, peer, sender):
        base, packed, quarter = at_of(kind)
        target = prefix if kind == 0 else suffix
        return pltpu.make_async_remote_copy(
            src_ref=c_send.at[min(kind, 1), peer, pl.ds(packed, quarter)],
            dst_ref=target.at[pl.ds(base + sender * quarter, quarter)],
            send_sem=c_send_sem.at[kind], recv_sem=c_recv_sem.at[kind],
            device_id=at_seq(level * PLANE + peer), device_id_type=MESH,
        )

    def mates(body):
        def one(i, carry):
            body(lax.rem(spot + i, PLANE))
            return carry

        lax.fori_loop(1, PLANE, one, 0)

    def later(kind, body):
        def one(i, carry):
            plane = level + i if kind == 0 else level - i

            @pl.when(jnp.logical_and(plane >= 0, plane < planes))
            def _():
                body(jnp.clip(plane, 0, planes - 1))

            return carry

        lax.fori_loop(1, planes, one, 0)

    def behind(kind):
        return level if kind == 0 else planes - 1 - level

    def rows_for(kind, count):
        return st_send.at[pl.ds(0, count * at_of(kind)[2])]

    def tiles(kind, body):
        packed, quarter = at_of(kind)[1:]

        def one(i, carry):
            body(pl.multiple_of(i * TILE, TILE), pl.ds(pl.multiple_of(packed + i * TILE, TILE), TILE))
            return carry

        lax.fori_loop(0, quarter // TILE, one, 0)

    def own_quarter(kind):
        base, packed, quarter = at_of(kind)
        source = st_send if kind == 0 else lg_send
        a_buf[min(kind, 1), spot, pl.ds(packed, quarter)] = source[pl.ds(base + spot * quarter, quarter)]

    def scan_open(kind):
        mates(lambda peer: a_copy(kind, peer, spot).start())
        own_quarter(kind)

    def scan_planes(kind):
        way = min(kind, 1)
        bulk(rows_for(kind, PLANE - 1), got=a_recv_sem.at[kind])

        def tile(_, here):
            total = a_buf[way, 0, here].astype(jnp.float32)
            for s in range(1, PLANE):
                total = total + a_buf[way, s, here].astype(jnp.float32)
            b_send[way, here] = total.astype(jnp.bfloat16)

        tiles(kind, tile)
        later(kind, lambda plane: b_copy(kind, plane, level).start())

    def scan_close(kind):
        base, packed, quarter = at_of(kind)
        way = min(kind, 1)
        target = prefix if kind == 0 else suffix
        for count in range(1, planes):

            @pl.when(behind(kind) == count)
            def _():
                bulk(rows_for(kind, count), got=b_recv_sem.at[kind])


        def tile(_, here):
            total = b_buf[way, 0, here].astype(jnp.float32)
            for z in range(1, planes):
                total = total + b_buf[way, z, here].astype(jnp.float32)
            for s in range(PLANE) if kind == 0 else range(PLANE - 1, -1, -1):
                c_send[way, s, here] = total.astype(jnp.bfloat16)
                total = total + a_buf[way, s, here].astype(jnp.float32)

        tiles(kind, tile)
        mates(lambda peer: c_copy(kind, peer, spot).start())
        target[pl.ds(base + spot * quarter, quarter)] = c_send[way, spot, pl.ds(packed, quarter)]

    def scan_end(kind):
        bulk(rows_for(kind, PLANE - 1), got=c_recv_sem.at[kind])

    def scan_sent(kind):
        bulk(rows_for(kind, PLANE - 1), sent=a_send_sem.at[kind])
        bulk(rows_for(kind, PLANE - 1), sent=c_send_sem.at[kind])
        for count in range(1, planes):

            @pl.when(planes - 1 - behind(kind) == count)
            def _():
                bulk(rows_for(kind, count), sent=b_send_sem.at[kind])

    def span_of(c):
        return pl.ds(pl.multiple_of(c * chunk, chunk), chunk)

    def piece(j, c, sems, target, own=False):
        span = span_of(c)
        return pltpu.make_async_remote_copy(
            src_ref=w_ref.at[span] if own else w_all.at[j, span],
            dst_ref=w_all.at[j, span],
            send_sem=sems, recv_sem=w_recv_sem.at[j, c],
            device_id=at_seq(target), device_id_type=MESH,
        )

    def to_y(j, c, own=False, slot=0):
        return piece(j, c, w_send_sem.at[slot], nbr_y, own)

    def to_inner(j, c, own=False):
        return piece(j, c, w_send_sem.at[1], inner, own)

    def to_outer(j, c, own=False, slot=2):
        return piece(j, c, w_send_sem.at[slot], outer, own)

    def landed(j, c):
        to_y(j, c).wait_recv()

    def own_piece(c):
        to_y(mine, c, True).start()
        to_inner(mine, c, True).start()

        @pl.when(middle)
        def _():
            to_outer(mine, c, True).start()

    turn = parts[0] + parts[1]

    def pump(phase, c):
        def move(j, ways):
            landed(j, c)
            for way in ways:
                way(j, c).start()

        if phase == 0:

            @pl.when(edge)
            def _():
                move(c0, (to_inner,))
                move(o1, (to_y,))

            @pl.when(middle)
            def _():
                move(o0, (to_inner,))
                move(o2, (to_outer, to_y))

        elif phase == 1:

            @pl.when(edge)
            def _():
                move(o2, (to_y,))

            @pl.when(middle)
            def _():
                move(o3, (to_outer, to_y))

        else:

            @pl.when(edge)
            def _():
                landed(o3, c)

                @pl.when(c == turn)
                def _():
                    to_y(o3, c, slot=3).start()

            @pl.when(middle)
            def _():
                landed(c3, c)

                @pl.when(c != turn)
                def _():
                    to_outer(c3, c, slot=3).start()

    def pieces_sent():
        bulk(w_all.at[pl.ds(0, 3)], sent=w_send_sem.at[0])
        bulk(w_all.at[pl.ds(0, 2)], sent=w_send_sem.at[1])

        @pl.when(middle)
        def _():
            bulk(w_all.at[pl.ds(0, 3)], sent=w_send_sem.at[2])
            bulk(w_all.at[0, pl.ds(0, (chunks - 1) * chunk)], sent=w_send_sem.at[3])

        @pl.when(edge)
        def _():
            bulk(w_all.at[0, pl.ds(0, chunk)], sent=w_send_sem.at[3])

    def settle(group, c):
        if group == 0:

            @pl.when(middle)
            def _():
                landed(c1, c)

        elif group == 1:
            landed(next_other, c)
        elif group == 2:
            landed(c2, c)
        else:

            @pl.when(edge)
            def _():
                landed(c3, c)

    causal = lower_mask(length)

    def score_step(h, carry):
        c = head_cols(h)
        kept = jnp.where(causal, contract_cols(q_ref[:, c], k_ref[:, c]), 0.0).astype(jnp.bfloat16)
        weights[h] = kept
        normed[h] = contract_mid(kept, v_ref[:, c])
        return carry

    def norm_step(h, carry):
        c = head_cols(h)
        numerator = normed[h] + contract_mid(q_ref[:, c], prefix[c])
        inv = 1.0 / jnp.sqrt(jnp.mean(numerator * numerator, axis=-1, keepdims=True) + 1e-06)
        value = numerator * inv
        normed[h] = value
        inv_spread[h] = jnp.broadcast_to(inv, (length, HEAD_DIM))
        att[own_rows, c] = value.astype(jnp.bfloat16)
        return carry

    def att_copy(i):
        c = span_of(i)
        return pltpu.make_async_remote_copy(
            src_ref=att.at[own_rows, c], dst_ref=att.at[far_rows, c],
            send_sem=t_sem.at[0], recv_sem=t_sem.at[1],
            device_id=at_seq(nbr_x), device_id_type=MESH,
        )

    def od_copy(c):
        return pltpu.make_async_remote_copy(
            src_ref=od_send.at[c], dst_ref=od_recv.at[c],
            send_sem=o_send_sem.at[0], recv_sem=o_recv_sem.at[c],
            device_id=at_seq(nbr_x), device_id_type=MESH,
        )

    def direction_step(group, c):
        span = span_of(c)
        total = None
        for j in groups[group]:
            term = contract_cols(g_all[j], w_all[j, span])
            total = term if total is None else total + term
        if group > 0:
            total = total + out_dir[:, span]
        if group < len(groups) - 1:
            out_dir[:, span] = total
        else:
            out_dir[own_rows, span] = total[:length]
            od_send[c] = total[length:].astype(jnp.bfloat16)
            od_copy(c).start()

    def p_copy(slot):
        return pltpu.make_async_remote_copy(
            src_ref=p_send.at[slot], dst_ref=p_recv.at[slot],
            send_sem=p_send_sem.at[0], recv_sem=p_recv_sem.at[slot],
            device_id=(me, other), device_id_type=MESH,
        )

    def m_copy(slot):
        return pltpu.make_async_remote_copy(
            src_ref=m_send.at[slot], dst_ref=m_recv.at[slot],
            send_sem=m_sem.at[0], recv_sem=m_sem.at[1],
            device_id=at_seq(nbr_x), device_id_type=MESH,
        )

    def partial_step(j):
        term = contract_mid(att[...], w_all[j]).astype(jnp.bfloat16)
        slot = lax.rem(j, half)

        @pl.when(j // half == core)
        def _():
            p_own[slot] = term

        @pl.when(j // half != core)
        def _():
            p_send[slot] = term
            p_copy(slot).start()

    def mixed_cols(slot, parity):
        return pl.ds(pl.multiple_of((slot * 2 + parity) * cols, cols), cols)

    def mix_step(slot, carry):
        p_copy(slot).wait_recv()
        both = (p_own[slot].astype(jnp.float32) + p_recv[slot].astype(jnp.float32)).astype(jnp.bfloat16)
        m_send[slot] = both[length:]
        m_copy(slot).start()
        mixed_ref[:, mixed_cols(slot, bit_x)] = both[:length]
        return carry

    def numer_step(h, carry):
        c = head_cols(h)
        sub = pl.ds(pl.multiple_of(lax.rem(h, chunk_heads) * HEAD_DIM, HEAD_DIM), HEAD_DIM)
        toward = out_dir[own_rows, c] + od_recv[h // chunk_heads, :, sub].astype(jnp.float32)
        unit = normed[h]
        along = jnp.mean(toward * unit, axis=-1, keepdims=True)
        low = ((toward - unit * along) * inv_spread[h]).astype(jnp.bfloat16)
        ng[:, c] = low
        lg_send[c] = contract_rows(q_ref[:, c], low).astype(jnp.bfloat16)
        return carry

    def numer_chunk(c):
        od_copy(c).wait_recv()
        lax.fori_loop(c * chunk_heads, (c + 1) * chunk_heads, numer_step, 0)

    def pair_step(h, carry):
        c = head_cols(h)
        low = ng[:, c]
        pair = jnp.where(causal, contract_cols(low, v_ref[:, c]), 0.0).astype(jnp.bfloat16)
        dq_ref[:, c] = (contract_mid(pair, k_ref[:, c]) + contract_cols(low, prefix[c])).astype(jnp.bfloat16)
        k_part[h] = contract_rows(pair, q_ref[:, c])
        v_part[h] = contract_rows(weights[h], low)
        return carry

    def each(count, body):
        def one(i, carry):
            body(i)
            return carry

        lax.fori_loop(0, count, one, 0)

    def heads_of(c, body):
        lax.fori_loop(c * chunk_heads, (c + 1) * chunk_heads, body, 0)

    def last_step(h, carry):
        c = head_cols(h)
        dk_ref[:, c] = (k_part[h] + contract_cols(v_ref[:, c], suffix[c])).astype(jnp.bfloat16)
        dv_ref[:, c] = (v_part[h] + contract_mid(k_ref[:, c], suffix[c])).astype(jnp.bfloat16)
        return carry

    def each(first, last, body):
        def one(i, carry):
            body(i)
            return carry

        lax.fori_loop(first, last, one, 0)

    def aim(group, first, last):
        def one(c):
            settle(group, c)
            direction_step(group, c)

        each(first, last, one)

    e1, e2, e3 = parts[0], parts[0] + parts[1], chunks

    pl.semaphore_wait(barrier, 2 * PLANE - 1)
    own_piece(0)
    for i in range(half):
        grad_core(i).start()
    grad_pair(0).start()
    for z in range(planes):

        @pl.when(z >= level)
        def _():
            b_buf[0, z] = jnp.zeros(b_buf.shape[2:], b_buf.dtype)

        @pl.when(z <= level)
        def _():
            b_buf[1, z] = jnp.zeros(b_buf.shape[2:], b_buf.dtype)

    k_load.wait()
    v_load.wait()
    team = heads // PLANE

    def some_states(peer):
        lax.fori_loop(peer * team, (peer + 1) * team, make_state, 0)

    def open_states(peer):
        some_states(peer)
        a_copy(0, peer, spot).start()

    mates(open_states)
    each(1, half, lambda i: grad_pair(i).start())
    each(1, e1, own_piece)
    some_states(spot)
    own_quarter(0)
    q_load.wait()
    lax.fori_loop(0, heads, score_step, 0)
    scan_planes(0)
    pump(0, 0)
    scan_close(0)
    each(1, e1, lambda c: pump(0, c))
    each(0, e1, lambda c: pump(1, c))
    some_grads = g_all.at[pl.ds(0, half), own_rows]
    bulk(some_grads, got=g_recv_sem.at[1])
    for i in range(half):
        grad_relay(i).start()
    own_w.wait()
    pltpu.make_async_copy(some_grads, some_grads, local_sem.at[4]).wait()
    bulk(some_grads, got=g_recv_sem.at[0])
    scan_end(0)

    def stage(c):
        heads_of(c, norm_step)
        att_copy(c).start()

    each(0, 4, stage)
    each(0, e1, lambda c: pump(2, c))
    each(e1, e2, own_piece)
    bulk(some_grads, got=g_recv_sem.at[2])
    each(4, chunks, lambda c: heads_of(c, norm_step))
    aim(0, 0, e1)
    aim(1, 0, e1)
    aim(2, 0, e1)
    aim(3, 0, e1)

    def stage(c):
        pump(0, c)
        att_copy(c - e1 + 4).start()

    each(e1, e2, stage)
    each(e2, e3, own_piece)
    each(e2 - e1 + 4, chunks, lambda c: att_copy(c).start())
    each(0, e1, numer_chunk)
    scan_open(1)
    each(e2, e3, lambda c: pump(0, c))

    def stage(c):
        pump(1, c)
        settle(0, c)
        direction_step(0, c)
        heads_of(c - e1, pair_step)

    each(e1, e2, stage)
    scan_planes(1)
    bulk(att.at[own_rows], got=t_sem.at[1])
    aim(0, e2, e3)
    partial_step(mine)
    partial_step(near_own)
    partial_step(near_other)
    aim(1, e1, e2)
    each(e2, e3, lambda c: settle(1, c))
    partial_step(next_other)
    pump(2, e1)
    near = level // (planes // 2)

    @pl.when(core == near)
    def _():
        lax.fori_loop(0, half, mix_step, 0)

    each(e1 + 1, e2 - 1, lambda c: pump(2, c))
    scan_close(1)
    each(e2 - 1, e2, lambda c: pump(2, c))
    each(e2, e3, lambda c: pump(1, c))
    each(e2, e3, lambda c: direction_step(1, c))
    partial_step(o2)
    aim(2, e1, e2)
    aim(3, e1, e2)
    scan_end(1)
    each(0, e1, lambda c: heads_of(c, last_step))
    each(e2, e3, lambda c: pump(2, c))
    aim(2, e2, e3)
    partial_step(o3)
    aim(3, e2, e3)
    each(e1, e2, numer_chunk)
    scan_open(2)
    partial_step(c2)
    each(e2, e3, numer_chunk)
    scan_open(3)
    partial_step(c3)
    scan_planes(2)
    scan_planes(3)

    @pl.when(core != near)
    def _():
        lax.fori_loop(0, half, mix_step, 0)

    scan_close(2)
    each(e1, e2, lambda c: heads_of(c, pair_step))
    scan_close(3)
    each(e2, e3, lambda c: heads_of(c, pair_step))
    scan_end(2)
    each(e1, e2, lambda c: heads_of(c, last_step))
    scan_end(3)
    each(e2, e3, lambda c: heads_of(c, last_step))

    def take_mixed(slot, carry):
        mixed_ref[:, mixed_cols(slot, 1 - bit_x)] = m_recv[slot]
        return carry

    bulk(m_recv, got=m_sem.at[1])
    lax.fori_loop(0, half, take_mixed, 0)

    pieces_sent()
    bulk(od_send, sent=o_send_sem.at[0])
    bulk(att.at[own_rows], sent=t_sem.at[0])
    bulk(p_send, sent=p_send_sem.at[0])
    bulk(m_send, sent=m_sem.at[0])
    for i in range(3):
        bulk(some_grads, sent=g_send_sem.at[i])
    for kind in range(len(parts) + 1):
        scan_sent(kind)


def store_kernel(*refs):
    count = (len(refs) - 1) // 2
    copies = [pltpu.make_async_copy(refs[i], refs[count + i], refs[-1].at[i]) for i in range(count)]
    for copy in copies:
        copy.start()
    for copy in copies:
        copy.wait()


def store(*arrays):
    count = len(arrays)
    return pl.pallas_call(
        store_kernel,
        out_shape=tuple(jax.ShapeDtypeStruct(a.shape, a.dtype) for a in arrays),
        in_specs=[pl.BlockSpec(memory_space=pltpu.VMEM)] * count,
        out_specs=(pl.BlockSpec(memory_space=pltpu.HBM),) * count,
        scratch_shapes=[pltpu.SemaphoreType.DMA((count,))],
        compiler_params=pltpu.CompilerParams(vmem_limit_bytes=8 * 2**20),
    )(*arrays)


def fused(blocks, queries, key_rows, values, out_weight, out_grad):
    length, width = queries.shape
    heads = width // HEAD_DIM
    rows, cols = out_weight.shape
    low, wide = jnp.bfloat16, jnp.float32
    size = blocks // 2
    half = size // 2
    chunks = sum(PARTS)
    state = pltpu.VMEM((rows, HEAD_DIM), low)
    fourth = rows // PLANE
    by_spot = pltpu.VMEM((2, PLANE, fourth, HEAD_DIM), low)
    by_head = pltpu.VMEM((heads, length, HEAD_DIM), wide)
    flat = pltpu.VMEM((length, width), low)
    parts = pltpu.VMEM((half, 2 * length, cols), low)
    shares = pltpu.VMEM((half, length, cols), low)
    steps = pltpu.VMEM((chunks, length, rows // chunks), low)
    dma = pltpu.SemaphoreType.DMA
    out = jax.ShapeDtypeStruct((length, width), low)
    vmem, in_hbm = pl.BlockSpec(memory_space=pltpu.VMEM), pl.BlockSpec(memory_space=pltpu.HBM)
    scans = dma((len(PARTS) + 1,))
    results = pl.pallas_call(
        functools.partial(kernel, blocks, chunks, PARTS),
        out_shape=(out, out, out, out),
        in_specs=[in_hbm] * 5,
        out_specs=(vmem, vmem, vmem, vmem),
        scratch_shapes=[
            flat, flat, flat,
            pltpu.VMEM((size, rows, cols), low),
            pltpu.VMEM((size, 2 * length, cols), low),
            state, state, state, state,
            by_spot, pltpu.VMEM((2, fourth, HEAD_DIM), low), by_spot, by_spot,
            pltpu.VMEM((2 * length, rows), wide),
            steps, steps,
            by_head, by_head,
            pltpu.VMEM((heads, length, length), low),
            pltpu.VMEM((2 * length, width), low),
            parts, parts, parts, shares, shares,
            flat, by_head, by_head,
            dma((size, chunks)), dma((4,)), dma((5,)), dma((3,)), dma((3,)),
            scans, scans, scans, scans, scans, scans,
            dma((1,)), dma((half,)), dma((2,)), dma((2,)), dma((1,)), dma((chunks,)),
        ],
        compiler_params=pltpu.CompilerParams(
            collective_id=0, has_side_effects=True, vmem_limit_bytes=49 * 2**20
        ),
    )(queries, key_rows, values, out_weight, out_grad)
    return store(*results)


def solution(mesh):
    blocks, cores = mesh.shape["seq"], mesh.shape["head"]

    def step(queries, key_rows, values, out_weight, out_grad):
        heads = queries.shape[1] // HEAD_DIM
        fits = cores == 2 and blocks == PLANE * PLANE and heads == blocks and out_weight.shape[1] % HEAD_DIM == 0
        fits = fits and out_weight.shape[0] == queries.shape[1] and out_weight.shape[0] % out_weight.shape[1] == 0
        if fits and out_weight.shape[1] * blocks == queries.shape[1] * cores:
            return fused(blocks, queries, key_rows, values, out_weight, out_grad)
        return per_device(queries, key_rows, values, out_weight, out_grad)

    placed = (
        P("seq", "head"),
        P("seq", "head"),
        P("seq", "head"),
        P("head", "seq"),
        P("seq", "head"),
    )
    return jax.shard_map(
        step,
        mesh=mesh,
        in_specs=placed,
        out_specs=(P("seq", "head"), P("seq", "head"), P("seq", "head"), P("seq", "head")),
        check_vma=False,
    )
```

```python
import functools

import jax
import jax.numpy as jnp
from jax import lax
from jax.experimental import pallas as pl
from jax.experimental.pallas import tpu as pltpu
from jax.sharding import PartitionSpec as P

HEAD_DIM = 128
MESH = pl.DeviceIdType.MESH
PLANE = 4
PARTS = (3, 3, 2)
TILE = 64
FOLDED = 1
EARLY = 2


def prefix_2(value, axis, combine, identity):
    length, position = (lax.axis_size(axis), lax.axis_index(axis))
    everything = lax.all_gather(value, axis)
    start = jnp.broadcast_to(jnp.asarray(identity, value.dtype), value.shape)

    def hop(k, before):
        reached = k < position
        new = combine(before, everything[k])
        return jnp.where(reached, new, before)

    return lax.fori_loop(0, length, hop, start)


def prefix_3(value, axis, combine, identity):
    length, position = (lax.axis_size(axis), lax.axis_index(axis))
    everything = lax.all_gather(value.astype(jnp.bfloat16), axis)
    start = jnp.broadcast_to(jnp.asarray(identity, value.dtype), value.shape)

    def hop(k, before):
        at = length - 1 - k
        reached = at > position
        new = combine(before, everything[at].astype(value.dtype))
        return jnp.where(reached, new, before)

    return lax.fori_loop(0, length, hop, start)


def lower_mask(length):
    row_ids = lax.broadcasted_iota(jnp.int32, (length, length), 0)
    col_ids = lax.broadcasted_iota(jnp.int32, (length, length), 1)
    return row_ids >= col_ids


def add_states(earlier, latter):
    return earlier + latter


def contract_cols(left_side, right_side):
    return lax.dot_general(
        left_side, right_side, (((1,), (1,)), ((), ())), preferred_element_type=jnp.float32
    )


def contract_rows(left_side, right_side):
    return lax.dot_general(
        left_side, right_side, (((0,), (0,)), ((), ())), preferred_element_type=jnp.float32
    )


def contract_mid(left_side, right_side):
    return jnp.dot(left_side, right_side, preferred_element_type=jnp.float32)


def per_device(queries, key_rows, values, out_weight, out_grad):
    length = queries.shape[0]
    heads_here = queries.shape[1] // HEAD_DIM
    query_heads = queries.reshape(length, heads_here, HEAD_DIM)
    key_heads = key_rows.reshape(length, heads_here, HEAD_DIM)
    value_heads = values.reshape(length, heads_here, HEAD_DIM)
    causal = lower_mask(length)[None]
    local_state = jnp.einsum(
        "shd,she->hde", key_heads, value_heads, preferred_element_type=jnp.float32
    )
    prefix = prefix_2(local_state, "seq", add_states, jnp.zeros_like(local_state))
    prefix_low = prefix.astype(jnp.bfloat16)
    scores = jnp.einsum("thd,shd->hts", query_heads, key_heads, preferred_element_type=jnp.float32)
    weights = jnp.where(causal, scores, 0.0).astype(jnp.bfloat16)
    numerator = jnp.einsum("hts,she->the", weights, value_heads, preferred_element_type=jnp.float32)
    numerator = numerator + jnp.einsum(
        "thd,hde->the", query_heads, prefix_low, preferred_element_type=jnp.float32
    )
    spread = jnp.sqrt(jnp.mean(numerator * numerator, axis=-1, keepdims=True) + 1e-06)
    normed = numerator / spread
    attended = normed.astype(jnp.bfloat16).reshape(length, heads_here * HEAD_DIM)
    full_weight = lax.all_gather(out_weight, "seq", axis=1, tiled=True)
    partial_value = jnp.dot(attended, full_weight, preferred_element_type=jnp.float32)
    layer_out = lax.psum_scatter(
        partial_value.astype(jnp.bfloat16), "head", scatter_dimension=1, tiled=True
    )
    out_dir = contract_cols(lax.all_gather(out_grad, "head", axis=1, tiled=True), full_weight)
    out_dir = out_dir.reshape(length, heads_here, HEAD_DIM)
    along_dir = jnp.mean(out_dir * normed, axis=-1, keepdims=True)
    numer_grad = ((out_dir - normed * along_dir) / spread).astype(jnp.bfloat16)
    local_grad = jnp.einsum(
        "thd,the->hde", query_heads, numer_grad, preferred_element_type=jnp.float32
    )
    suffix = prefix_3(local_grad, "seq", add_states, jnp.zeros_like(local_grad))
    suffix_low = suffix.astype(jnp.bfloat16)
    pair_scores = jnp.einsum(
        "the,she->hts", numer_grad, value_heads, preferred_element_type=jnp.float32
    )
    pair_low = jnp.where(causal, pair_scores, 0.0).astype(jnp.bfloat16)
    query_out = jnp.einsum("hts,shd->thd", pair_low, key_heads, preferred_element_type=jnp.float32)
    query_out = query_out + jnp.einsum(
        "the,hde->thd", numer_grad, prefix_low, preferred_element_type=jnp.float32
    )
    key_out = jnp.einsum("hts,thd->shd", pair_low, query_heads, preferred_element_type=jnp.float32)
    key_out = key_out + jnp.einsum(
        "she,hde->shd", value_heads, suffix_low, preferred_element_type=jnp.float32
    )
    value_out = jnp.einsum("hts,the->she", weights, numer_grad, preferred_element_type=jnp.float32)
    value_out = value_out + jnp.einsum(
        "shd,hde->she", key_heads, suffix_low, preferred_element_type=jnp.float32
    )
    flat_shape = (length, heads_here * HEAD_DIM)
    return (
        layer_out,
        query_out.reshape(flat_shape).astype(jnp.bfloat16),
        key_out.reshape(flat_shape).astype(jnp.bfloat16),
        value_out.reshape(flat_shape).astype(jnp.bfloat16),
    )


def kernel(
    blocks, chunks, parts, q_in, k_in, v_in, w_ref, g_ref,
    mixed_ref, dq_ref, dk_ref, dv_ref,
    q_ref, k_ref, v_ref, w_all, g_all, st_send, prefix, lg_send, suffix, a_buf, b_send, b_buf, c_send,
    out_dir, od_send, od_recv, normed, inv_spread, weights, att, p_own, p_send, p_recv, m_send, m_recv,
    ng, k_part, v_part,
    w_recv_sem, w_send_sem, local_sem, g_send_sem, g_recv_sem,
    a_send_sem, a_recv_sem, b_send_sem, b_recv_sem, c_send_sem, c_recv_sem,
    p_send_sem, p_recv_sem, m_sem, t_sem, o_send_sem, o_recv_sem,
):
    me = lax.axis_index("seq")
    core = lax.axis_index("head")
    other = 1 - core
    planes = blocks // PLANE
    size = blocks // 2
    spot = lax.rem(me, PLANE)
    level = me // PLANE
    bit_x, bit_y = lax.rem(spot, 2), spot // 2
    length, width = q_ref.shape
    heads = width // HEAD_DIM
    rows, cols = w_ref.shape
    chunk = rows // chunks
    chunk_heads = chunk // HEAD_DIM
    lower = level < planes // 2
    middle = jnp.where(lower, level, planes - 1 - level) > 0
    edge = jnp.logical_not(middle)
    nbr_x = me + 1 - 2 * bit_x
    nbr_y = me + 2 - 4 * bit_y
    step_in = jnp.where(lower, PLANE, -PLANE)
    inner = me + step_in
    outer = jnp.where(middle, me - step_in, inner)

    def at_seq(position):
        return (position, core)

    def own_col(k):
        return jnp.where(lower, k, planes - 1 - k) * 2 + bit_y

    def other_col(k):
        return jnp.where(lower, k, planes - 1 - k) * 2 + 1 - bit_y

    o0, o1, o2, o3 = (own_col(k) for k in range(4))
    c0, c1, c2, c3 = (other_col(k) for k in range(4))
    mine = me // 2
    near_own = jnp.where(middle, o0, o1)
    near_other, next_other = jnp.where(middle, c1, c0), jnp.where(middle, c0, c1)
    groups = ((mine, near_own, near_other), (o2, next_other), (o3, c2), (c3,))

    q_load = pltpu.make_async_copy(q_in, q_ref, local_sem.at[0])
    k_load = pltpu.make_async_copy(k_in, k_ref, local_sem.at[1])
    v_load = pltpu.make_async_copy(v_in, v_ref, local_sem.at[2])
    own_w = pltpu.make_async_copy(w_ref, w_all.at[mine], local_sem.at[3])
    k_load.start()
    v_load.start()
    barrier = pltpu.get_barrier_semaphore()

    def greet(i, carry):
        for mate in (level * PLANE + lax.rem(spot + i, PLANE), lax.rem(level + i, planes) * PLANE + spot):
            pl.semaphore_signal(barrier, inc=1, device_id=at_seq(mate), device_id_type=MESH)
        return carry

    lax.fori_loop(1, PLANE, greet, 0)
    pl.semaphore_signal(barrier, inc=1, device_id=(me, other), device_id_type=MESH)

    half = size // 2
    own_rows, far_rows = pl.ds(0, length), pl.ds(length, length)

    def bulk(ref, sent=None, got=None):
        copy = pltpu.make_async_remote_copy(
            src_ref=ref, dst_ref=ref,
            send_sem=got if sent is None else sent, recv_sem=sent if got is None else got,
            device_id=(me, other), device_id_type=MESH,
        )
        copy.wait_recv() if sent is None else copy.wait_send()

    def grad_cols(j, parity):
        return pl.ds(pl.multiple_of((lax.rem(j, half) * 2 + parity) * cols, cols), cols)

    def own_grad(i):
        j = core * half + i
        return pltpu.make_async_copy(g_ref.at[:, grad_cols(j, bit_x)], g_all.at[j, own_rows], local_sem.at[4])

    def grad_core(i):
        j = core * half + i
        return pltpu.make_async_remote_copy(
            src_ref=g_ref.at[:, grad_cols(j, bit_x)], dst_ref=g_all.at[j, own_rows],
            send_sem=g_send_sem.at[0], recv_sem=g_recv_sem.at[0],
            device_id=(me, other), device_id_type=MESH,
        )

    def grad_pair(i):
        j = core * half + i
        return pltpu.make_async_remote_copy(
            src_ref=g_ref.at[:, grad_cols(j, 1 - bit_x)], dst_ref=g_all.at[j, far_rows],
            send_sem=g_send_sem.at[1], recv_sem=g_recv_sem.at[1],
            device_id=at_seq(nbr_x), device_id_type=MESH,
        )

    def grad_relay(i):
        j = core * half + i
        return pltpu.make_async_remote_copy(
            src_ref=g_all.at[j, far_rows], dst_ref=g_all.at[j, far_rows],
            send_sem=g_send_sem.at[2], recv_sem=g_recv_sem.at[2],
            device_id=(me, other), device_id_type=MESH,
        )

    q_load.start()
    own_w.start()
    for i in range(half):
        own_grad(i).start()
    def head_cols(h):
        return pl.ds(pl.multiple_of(h * HEAD_DIM, HEAD_DIM), HEAD_DIM)

    def make_state(h, carry):
        c = head_cols(h)
        st_send[c] = contract_rows(k_ref[:, c], v_ref[:, c]).astype(jnp.bfloat16)
        return carry

    def at_of(kind):
        first, count = (0, chunks) if kind == 0 else (sum(parts[: kind - 1]), parts[kind - 1])
        quarter = count * chunk // PLANE
        return first * chunk, first * chunk // PLANE, quarter

    def a_copy(kind, peer, sender):
        base, packed, quarter = at_of(kind)
        source = st_send if kind == 0 else lg_send
        return pltpu.make_async_remote_copy(
            src_ref=source.at[pl.ds(base + peer * quarter, quarter)],
            dst_ref=a_buf.at[min(kind, 1), sender, pl.ds(packed, quarter)],
            send_sem=a_send_sem.at[kind], recv_sem=a_recv_sem.at[kind],
            device_id=at_seq(level * PLANE + peer), device_id_type=MESH,
        )

    def b_copy(kind, plane, sender):
        packed, quarter = at_of(kind)[1:]
        return pltpu.make_async_remote_copy(
            src_ref=b_send.at[min(kind, 1), pl.ds(packed, quarter)],
            dst_ref=b_buf.at[min(kind, 1), sender, pl.ds(packed, quarter)],
            send_sem=b_send_sem.at[kind], recv_sem=b_recv_sem.at[kind],
            device_id=at_seq(plane * PLANE + spot), device_id_type=MESH,
        )

    def c_copy(kind, peer, sender):
        base, packed, quarter = at_of(kind)
        target = prefix if kind == 0 else suffix
        return pltpu.make_async_remote_copy(
            src_ref=c_send.at[min(kind, 1), peer, pl.ds(packed, quarter)],
            dst_ref=target.at[pl.ds(base + sender * quarter, quarter)],
            send_sem=c_send_sem.at[kind], recv_sem=c_recv_sem.at[kind],
            device_id=at_seq(level * PLANE + peer), device_id_type=MESH,
        )

    def mates(body):
        def one(i, carry):
            body(lax.rem(spot + i, PLANE))
            return carry

        lax.fori_loop(1, PLANE, one, 0)

    def later(kind, body):
        def one(i, carry):
            plane = level + i if kind == 0 else level - planes + i

            @pl.when(jnp.logical_and(plane >= 0, plane < planes))
            def _():
                body(jnp.clip(plane, 0, planes - 1))

            return carry

        lax.fori_loop(1, planes, one, 0)

    def behind(kind):
        return level if kind == 0 else planes - 1 - level

    def rows_for(kind, count):
        return st_send.at[pl.ds(0, count * at_of(kind)[2])]

    def tiles(kind, body):
        packed, quarter = at_of(kind)[1:]

        def one(i, carry):
            body(pl.multiple_of(i * TILE, TILE), pl.ds(pl.multiple_of(packed + i * TILE, TILE), TILE))
            return carry

        lax.fori_loop(0, quarter // TILE, one, 0)

    def own_quarter(kind):
        base, packed, quarter = at_of(kind)
        source = st_send if kind == 0 else lg_send
        a_buf[min(kind, 1), spot, pl.ds(packed, quarter)] = source[pl.ds(base + spot * quarter, quarter)]

    def scan_open(kind):
        mates(lambda peer: a_copy(kind, peer, spot).start())
        own_quarter(kind)

    def scan_planes(kind):
        way = min(kind, 1)
        bulk(rows_for(kind, PLANE - 1), got=a_recv_sem.at[kind])

        def tile(_, here):
            total = a_buf[way, 0, here].astype(jnp.float32)
            for s in range(1, PLANE):
                total = total + a_buf[way, s, here].astype(jnp.float32)
            b_send[way, here] = total.astype(jnp.bfloat16)

        tiles(kind, tile)
        later(kind, lambda plane: b_copy(kind, plane, level).start())

    def scan_close(kind):
        base, packed, quarter = at_of(kind)
        way = min(kind, 1)
        target = prefix if kind == 0 else suffix
        for count in range(1, planes):

            @pl.when(behind(kind) == count)
            def _():
                bulk(rows_for(kind, count), got=b_recv_sem.at[kind])


        def tile(_, here):
            total = b_buf[way, 0, here].astype(jnp.float32)
            for z in range(1, planes):
                total = total + b_buf[way, z, here].astype(jnp.float32)
            for s in range(PLANE) if kind == 0 else range(PLANE - 1, -1, -1):
                c_send[way, s, here] = total.astype(jnp.bfloat16)
                total = total + a_buf[way, s, here].astype(jnp.float32)

        tiles(kind, tile)
        mates(lambda peer: c_copy(kind, peer, spot).start())
        target[pl.ds(base + spot * quarter, quarter)] = c_send[way, spot, pl.ds(packed, quarter)]

    def scan_end(kind):
        bulk(rows_for(kind, PLANE - 1), got=c_recv_sem.at[kind])

    def scan_sent(kind):
        bulk(rows_for(kind, PLANE - 1), sent=a_send_sem.at[kind])
        bulk(rows_for(kind, PLANE - 1), sent=c_send_sem.at[kind])
        for count in range(1, planes):

            @pl.when(planes - 1 - behind(kind) == count)
            def _():
                bulk(rows_for(kind, count), sent=b_send_sem.at[kind])

    def span_of(c):
        return pl.ds(pl.multiple_of(c * chunk, chunk), chunk)

    def piece(j, c, sems, target, own=False):
        span = span_of(c)
        return pltpu.make_async_remote_copy(
            src_ref=w_ref.at[span] if own else w_all.at[j, span],
            dst_ref=w_all.at[j, span],
            send_sem=sems, recv_sem=w_recv_sem.at[j, c],
            device_id=at_seq(target), device_id_type=MESH,
        )

    def to_y(j, c, own=False, slot=0):
        return piece(j, c, w_send_sem.at[slot], nbr_y, own)

    def to_inner(j, c, own=False):
        return piece(j, c, w_send_sem.at[1], inner, own)

    def to_outer(j, c, own=False, slot=2):
        return piece(j, c, w_send_sem.at[slot], outer, own)

    def landed(j, c):
        to_y(j, c).wait_recv()

    def own_piece(c):
        to_y(mine, c, True).start()
        to_inner(mine, c, True).start()

        @pl.when(middle)
        def _():
            to_outer(mine, c, True).start()

    turns = parts[0], parts[0] + parts[1]

    def by_y(c):
        return jnp.logical_or(c == turns[0], c == turns[1])

    def pump(phase, c):
        def move(j, ways):
            landed(j, c)
            for way in ways:
                way(j, c).start()

        if phase == 0:

            @pl.when(edge)
            def _():
                move(c0, (to_inner,))
                move(o1, (to_y,))

            @pl.when(middle)
            def _():
                move(o0, (to_inner,))
                move(o2, (to_outer, to_y))

        elif phase == 1:

            @pl.when(edge)
            def _():
                move(o2, (to_y,))

            @pl.when(middle)
            def _():
                move(o3, (to_outer, to_y))

        else:

            @pl.when(edge)
            def _():
                landed(o3, c)

                @pl.when(by_y(c))
                def _():
                    to_y(o3, c, slot=3).start()

            @pl.when(middle)
            def _():
                landed(c3, c)

                @pl.when(jnp.logical_not(by_y(c)))
                def _():
                    to_outer(c3, c, slot=3).start()

    def pieces_sent():
        bulk(w_all.at[pl.ds(0, 3)], sent=w_send_sem.at[0])
        bulk(w_all.at[pl.ds(0, 2)], sent=w_send_sem.at[1])

        @pl.when(middle)
        def _():
            bulk(w_all.at[pl.ds(0, 3)], sent=w_send_sem.at[2])
            bulk(w_all.at[0, pl.ds(0, (chunks - len(turns)) * chunk)], sent=w_send_sem.at[3])

        @pl.when(edge)
        def _():
            bulk(w_all.at[0, pl.ds(0, len(turns) * chunk)], sent=w_send_sem.at[3])

    def settle(group, c):
        if group == 0:

            @pl.when(middle)
            def _():
                landed(c1, c)

        elif group == 1:
            landed(next_other, c)
        elif group == 2:
            landed(c2, c)
        else:

            @pl.when(edge)
            def _():
                landed(c3, c)

    causal = lower_mask(length)

    def score_step(h, carry):
        c = head_cols(h)
        kept = jnp.where(causal, contract_cols(q_ref[:, c], k_ref[:, c]), 0.0).astype(jnp.bfloat16)
        weights[h] = kept
        normed[h] = contract_mid(kept, v_ref[:, c])
        return carry

    def norm_step(h, carry):
        c = head_cols(h)
        numerator = normed[h] + contract_mid(q_ref[:, c], prefix[c])
        inv = 1.0 / jnp.sqrt(jnp.mean(numerator * numerator, axis=-1, keepdims=True) + 1e-06)
        value = numerator * inv
        normed[h] = value
        inv_spread[h] = jnp.broadcast_to(inv, (length, HEAD_DIM))
        att[own_rows, c] = value.astype(jnp.bfloat16)
        return carry

    def att_copy(i):
        c = span_of(i)
        return pltpu.make_async_remote_copy(
            src_ref=att.at[own_rows, c], dst_ref=att.at[far_rows, c],
            send_sem=t_sem.at[0], recv_sem=t_sem.at[1],
            device_id=at_seq(nbr_x), device_id_type=MESH,
        )

    def od_copy(c):
        return pltpu.make_async_remote_copy(
            src_ref=od_send.at[c], dst_ref=od_recv.at[c],
            send_sem=o_send_sem.at[0], recv_sem=o_recv_sem.at[c],
            device_id=at_seq(nbr_x), device_id_type=MESH,
        )

    def direction_step(group, c):
        span = span_of(c)
        total = None
        for j in groups[group]:
            term = contract_cols(g_all[j], w_all[j, span])
            total = term if total is None else total + term
        if group > 0:
            total = total + out_dir[:, span]
        if group < len(groups) - 1:
            out_dir[:, span] = total
        else:
            out_dir[own_rows, span] = total[:length]
            od_send[c] = total[length:].astype(jnp.bfloat16)
            od_copy(c).start()

    def p_copy(slot):
        return pltpu.make_async_remote_copy(
            src_ref=p_send.at[slot], dst_ref=p_recv.at[slot],
            send_sem=p_send_sem.at[0], recv_sem=p_recv_sem.at[slot],
            device_id=(me, other), device_id_type=MESH,
        )

    def m_copy(slot):
        return pltpu.make_async_remote_copy(
            src_ref=m_send.at[slot], dst_ref=m_recv.at[slot],
            send_sem=m_sem.at[0], recv_sem=m_sem.at[1],
            device_id=at_seq(nbr_x), device_id_type=MESH,
        )

    def partial_step(j):
        term = contract_mid(att[...], w_all[j]).astype(jnp.bfloat16)
        slot = lax.rem(j, half)

        @pl.when(j // half == core)
        def _():
            p_own[slot] = term

        @pl.when(j // half != core)
        def _():
            p_send[slot] = term
            p_copy(slot).start()

    def mixed_cols(slot, parity):
        return pl.ds(pl.multiple_of((slot * 2 + parity) * cols, cols), cols)

    def mix_step(slot, carry):
        p_copy(slot).wait_recv()
        both = (p_own[slot].astype(jnp.float32) + p_recv[slot].astype(jnp.float32)).astype(jnp.bfloat16)
        m_send[slot] = both[length:]
        m_copy(slot).start()
        mixed_ref[:, mixed_cols(slot, bit_x)] = both[:length]
        return carry

    def numer_step(h, carry):
        c = head_cols(h)
        sub = pl.ds(pl.multiple_of(lax.rem(h, chunk_heads) * HEAD_DIM, HEAD_DIM), HEAD_DIM)
        toward = out_dir[own_rows, c] + od_recv[h // chunk_heads, :, sub].astype(jnp.float32)
        unit = normed[h]
        along = jnp.mean(toward * unit, axis=-1, keepdims=True)
        low = ((toward - unit * along) * inv_spread[h]).astype(jnp.bfloat16)
        ng[:, c] = low
        lg_send[c] = contract_rows(q_ref[:, c], low).astype(jnp.bfloat16)
        return carry

    def numer_chunk(c):
        od_copy(c).wait_recv()
        lax.fori_loop(c * chunk_heads, (c + 1) * chunk_heads, numer_step, 0)

    def pair_step(h, carry):
        c = head_cols(h)
        low = ng[:, c]
        pair = jnp.where(causal, contract_cols(low, v_ref[:, c]), 0.0).astype(jnp.bfloat16)
        dq_ref[:, c] = (contract_mid(pair, k_ref[:, c]) + contract_cols(low, prefix[c])).astype(jnp.bfloat16)
        k_part[h] = contract_rows(pair, q_ref[:, c])
        v_part[h] = contract_rows(weights[h], low)
        return carry

    def each(count, body):
        def one(i, carry):
            body(i)
            return carry

        lax.fori_loop(0, count, one, 0)

    def heads_of(c, body):
        lax.fori_loop(c * chunk_heads, (c + 1) * chunk_heads, body, 0)

    def last_step(h, carry):
        c = head_cols(h)
        dk_ref[:, c] = (k_part[h] + contract_cols(v_ref[:, c], suffix[c])).astype(jnp.bfloat16)
        dv_ref[:, c] = (v_part[h] + contract_mid(k_ref[:, c], suffix[c])).astype(jnp.bfloat16)
        return carry

    def each(first, last, body):
        def one(i, carry):
            body(i)
            return carry

        lax.fori_loop(first, last, one, 0)

    def aim(group, first, last):
        def one(c):
            settle(group, c)
            direction_step(group, c)

        each(first, last, one)

    e1, e2, e3 = parts[0], parts[0] + parts[1], chunks

    pl.semaphore_wait(barrier, 2 * PLANE - 1)
    own_piece(0)
    for i in range(half):
        grad_core(i).start()
    grad_pair(0).start()
    for z in range(planes):

        @pl.when(z >= level)
        def _():
            b_buf[0, z] = jnp.zeros(b_buf.shape[2:], b_buf.dtype)

        @pl.when(z <= level)
        def _():
            b_buf[1, z] = jnp.zeros(b_buf.shape[2:], b_buf.dtype)

    k_load.wait()
    v_load.wait()
    team = heads // PLANE

    def some_states(peer):
        lax.fori_loop(peer * team, (peer + 1) * team, make_state, 0)

    def open_states(peer):
        some_states(peer)
        a_copy(0, peer, spot).start()

    mates(open_states)
    each(1, half, lambda i: grad_pair(i).start())
    each(1, e1, own_piece)
    some_states(spot)
    own_quarter(0)
    q_load.wait()
    lax.fori_loop(0, heads, score_step, 0)
    scan_planes(0)
    pump(0, 0)
    scan_close(0)
    each(1, e1, lambda c: pump(0, c))
    each(0, e1, lambda c: pump(1, c))
    each(e1, e2, own_piece)
    some_grads = g_all.at[pl.ds(0, half), own_rows]
    bulk(some_grads, got=g_recv_sem.at[1])
    for i in range(half):
        grad_relay(i).start()
    own_w.wait()
    pltpu.make_async_copy(some_grads, some_grads, local_sem.at[4]).wait()
    bulk(some_grads, got=g_recv_sem.at[0])
    scan_end(0)

    def stage(c):
        heads_of(c, norm_step)
        att_copy(c).start()

    each(0, 4, stage)
    each(0, e1, lambda c: pump(2, c))
    bulk(some_grads, got=g_recv_sem.at[2])
    each(4, chunks, lambda c: heads_of(c, norm_step))
    aim(0, 0, e1)
    aim(1, 0, e1)
    aim(2, 0, e1)
    aim(3, 0, e1)

    def stage(c):
        pump(0, c)
        att_copy(c - e1 + 4).start()

    each(e1, e2, stage)
    each(e2, e3, own_piece)
    each(e2 - e1 + 4, chunks, lambda c: att_copy(c).start())
    each(0, e1, numer_chunk)
    scan_open(1)
    each(e2, e3, lambda c: pump(0, c))

    def stage(c):
        pump(1, c)
        settle(0, c)
        direction_step(0, c)
        heads_of(c - e1, pair_step)

    each(e1, e2, stage)
    scan_planes(1)
    bulk(att.at[own_rows], got=t_sem.at[1])
    aim(0, e2, e3)
    partial_step(mine)
    partial_step(near_own)
    partial_step(near_other)
    aim(1, e1, e2)
    each(e2, e3, lambda c: settle(1, c))
    partial_step(next_other)
    pump(2, e1)
    near = level // (planes // 2)

    @pl.when(core == near)
    def _():
        lax.fori_loop(0, half, mix_step, 0)

    each(e1 + 1, e2 - 1, lambda c: pump(2, c))
    scan_close(1)
    each(e2 - 1, e2, lambda c: pump(2, c))
    each(e2, e3, lambda c: pump(1, c))
    each(e2, e3, lambda c: direction_step(1, c))
    partial_step(o2)
    aim(2, e1, e2)
    aim(3, e1, e2)
    scan_end(1)
    each(0, e1, lambda c: heads_of(c, last_step))
    each(e2, e3, lambda c: pump(2, c))
    aim(2, e2, e3)
    partial_step(o3)
    aim(3, e2, e3)
    each(e1, e2, numer_chunk)
    scan_open(2)
    partial_step(c2)

    def far_mix(*blocks_done):
        @pl.when(core != near)
        def _():
            for j in blocks_done:
                mix_step(lax.rem(j, half), 0)

    each(e2, e3, numer_chunk)
    scan_open(3)
    far_mix(o2, o3)
    partial_step(c3)
    scan_planes(2)
    scan_planes(3)

    @pl.when(level == planes - 1)
    def _():
        scan_close(2)
        scan_close(3)

    far_mix(c2, c3)
    each(e1, e3, lambda c: heads_of(c, pair_step))
    @pl.when(level < planes - 1)
    def _():
        scan_close(2)
        scan_close(3)

    scan_end(2)
    each(e1, e2, lambda c: heads_of(c, last_step))
    scan_end(3)
    each(e2, e3, lambda c: heads_of(c, last_step))

    def take_mixed(slot, carry):
        mixed_ref[:, mixed_cols(slot, 1 - bit_x)] = m_recv[slot]
        return carry

    bulk(m_recv, got=m_sem.at[1])
    lax.fori_loop(0, half, take_mixed, 0)

    pieces_sent()
    bulk(od_send, sent=o_send_sem.at[0])
    bulk(att.at[own_rows], sent=t_sem.at[0])
    bulk(p_send, sent=p_send_sem.at[0])
    bulk(m_send, sent=m_sem.at[0])
    for i in range(3):
        bulk(some_grads, sent=g_send_sem.at[i])
    for kind in range(len(parts) + 1):
        scan_sent(kind)


def store_kernel(*refs):
    count = (len(refs) - 1) // 2
    copies = [pltpu.make_async_copy(refs[i], refs[count + i], refs[-1].at[i]) for i in range(count)]
    for copy in copies:
        copy.start()
    for copy in copies:
        copy.wait()


def store(*arrays):
    count = len(arrays)
    return pl.pallas_call(
        store_kernel,
        out_shape=tuple(jax.ShapeDtypeStruct(a.shape, a.dtype) for a in arrays),
        in_specs=[pl.BlockSpec(memory_space=pltpu.VMEM)] * count,
        out_specs=(pl.BlockSpec(memory_space=pltpu.HBM),) * count,
        scratch_shapes=[pltpu.SemaphoreType.DMA((count,))],
        compiler_params=pltpu.CompilerParams(vmem_limit_bytes=8 * 2**20),
    )(*arrays)


def fused(blocks, queries, key_rows, values, out_weight, out_grad):
    length, width = queries.shape
    heads = width // HEAD_DIM
    rows, cols = out_weight.shape
    low, wide = jnp.bfloat16, jnp.float32
    size = blocks // 2
    half = size // 2
    chunks = sum(PARTS)
    state = pltpu.VMEM((rows, HEAD_DIM), low)
    fourth = rows // PLANE
    by_spot = pltpu.VMEM((2, PLANE, fourth, HEAD_DIM), low)
    by_head = pltpu.VMEM((heads, length, HEAD_DIM), wide)
    flat = pltpu.VMEM((length, width), low)
    parts = pltpu.VMEM((half, 2 * length, cols), low)
    shares = pltpu.VMEM((half, length, cols), low)
    steps = pltpu.VMEM((chunks, length, rows // chunks), low)
    dma = pltpu.SemaphoreType.DMA
    out = jax.ShapeDtypeStruct((length, width), low)
    vmem, in_hbm = pl.BlockSpec(memory_space=pltpu.VMEM), pl.BlockSpec(memory_space=pltpu.HBM)
    scans = dma((len(PARTS) + 1,))
    results = pl.pallas_call(
        functools.partial(kernel, blocks, chunks, PARTS),
        out_shape=(out, out, out, out),
        in_specs=[in_hbm] * 5,
        out_specs=(vmem, vmem, vmem, vmem),
        scratch_shapes=[
            flat, flat, flat,
            pltpu.VMEM((size, rows, cols), low),
            pltpu.VMEM((size, 2 * length, cols), low),
            state, state, state, state,
            by_spot, pltpu.VMEM((2, fourth, HEAD_DIM), low), by_spot, by_spot,
            pltpu.VMEM((2 * length, rows), wide),
            steps, steps,
            by_head, by_head,
            pltpu.VMEM((heads, length, length), low),
            pltpu.VMEM((2 * length, width), low),
            parts, parts, parts, shares, shares,
            flat, by_head, by_head,
            dma((size, chunks)), dma((4,)), dma((5,)), dma((3,)), dma((3,)),
            scans, scans, scans, scans, scans, scans,
            dma((1,)), dma((half,)), dma((2,)), dma((2,)), dma((1,)), dma((chunks,)),
        ],
        compiler_params=pltpu.CompilerParams(
            collective_id=0, has_side_effects=True, vmem_limit_bytes=49 * 2**20
        ),
    )(queries, key_rows, values, out_weight, out_grad)
    return store(*results)


def solution(mesh):
    blocks, cores = mesh.shape["seq"], mesh.shape["head"]

    def step(queries, key_rows, values, out_weight, out_grad):
        heads = queries.shape[1] // HEAD_DIM
        fits = cores == 2 and blocks == PLANE * PLANE and heads == blocks and out_weight.shape[1] % HEAD_DIM == 0
        fits = fits and out_weight.shape[0] == queries.shape[1] and out_weight.shape[0] % out_weight.shape[1] == 0
        if fits and out_weight.shape[1] * blocks == queries.shape[1] * cores:
            return fused(blocks, queries, key_rows, values, out_weight, out_grad)
        return per_device(queries, key_rows, values, out_weight, out_grad)

    placed = (
        P("seq", "head"),
        P("seq", "head"),
        P("seq", "head"),
        P("head", "seq"),
        P("seq", "head"),
    )
    return jax.shard_map(
        step,
        mesh=mesh,
        in_specs=placed,
        out_specs=(P("seq", "head"), P("seq", "head"), P("seq", "head"), P("seq", "head")),
        check_vma=False,
    )
```

```python
import functools

import jax
import jax.numpy as jnp
from jax import lax
from jax.experimental import pallas as pl
from jax.experimental.pallas import tpu as pltpu
from jax.sharding import PartitionSpec as P

HEAD_DIM = 128
MESH = pl.DeviceIdType.MESH
PLANE = 4
PARTS = (3, 3, 2)
TILE = 64
FOLDED = 1
EARLY = 2


def prefix_2(value, axis, combine, identity):
    length, position = (lax.axis_size(axis), lax.axis_index(axis))
    everything = lax.all_gather(value, axis)
    start = jnp.broadcast_to(jnp.asarray(identity, value.dtype), value.shape)

    def hop(k, before):
        reached = k < position
        new = combine(before, everything[k])
        return jnp.where(reached, new, before)

    return lax.fori_loop(0, length, hop, start)


def prefix_3(value, axis, combine, identity):
    length, position = (lax.axis_size(axis), lax.axis_index(axis))
    everything = lax.all_gather(value.astype(jnp.bfloat16), axis)
    start = jnp.broadcast_to(jnp.asarray(identity, value.dtype), value.shape)

    def hop(k, before):
        at = length - 1 - k
        reached = at > position
        new = combine(before, everything[at].astype(value.dtype))
        return jnp.where(reached, new, before)

    return lax.fori_loop(0, length, hop, start)


def lower_mask(length):
    row_ids = lax.broadcasted_iota(jnp.int32, (length, length), 0)
    col_ids = lax.broadcasted_iota(jnp.int32, (length, length), 1)
    return row_ids >= col_ids


def add_states(earlier, latter):
    return earlier + latter


def contract_cols(left_side, right_side):
    return lax.dot_general(
        left_side, right_side, (((1,), (1,)), ((), ())), preferred_element_type=jnp.float32
    )


def contract_rows(left_side, right_side):
    return lax.dot_general(
        left_side, right_side, (((0,), (0,)), ((), ())), preferred_element_type=jnp.float32
    )


def contract_mid(left_side, right_side):
    return jnp.dot(left_side, right_side, preferred_element_type=jnp.float32)


def per_device(queries, key_rows, values, out_weight, out_grad):
    length = queries.shape[0]
    heads_here = queries.shape[1] // HEAD_DIM
    query_heads = queries.reshape(length, heads_here, HEAD_DIM)
    key_heads = key_rows.reshape(length, heads_here, HEAD_DIM)
    value_heads = values.reshape(length, heads_here, HEAD_DIM)
    causal = lower_mask(length)[None]
    local_state = jnp.einsum(
        "shd,she->hde", key_heads, value_heads, preferred_element_type=jnp.float32
    )
    prefix = prefix_2(local_state, "seq", add_states, jnp.zeros_like(local_state))
    prefix_low = prefix.astype(jnp.bfloat16)
    scores = jnp.einsum("thd,shd->hts", query_heads, key_heads, preferred_element_type=jnp.float32)
    weights = jnp.where(causal, scores, 0.0).astype(jnp.bfloat16)
    numerator = jnp.einsum("hts,she->the", weights, value_heads, preferred_element_type=jnp.float32)
    numerator = numerator + jnp.einsum(
        "thd,hde->the", query_heads, prefix_low, preferred_element_type=jnp.float32
    )
    spread = jnp.sqrt(jnp.mean(numerator * numerator, axis=-1, keepdims=True) + 1e-06)
    normed = numerator / spread
    attended = normed.astype(jnp.bfloat16).reshape(length, heads_here * HEAD_DIM)
    full_weight = lax.all_gather(out_weight, "seq", axis=1, tiled=True)
    partial_value = jnp.dot(attended, full_weight, preferred_element_type=jnp.float32)
    layer_out = lax.psum_scatter(
        partial_value.astype(jnp.bfloat16), "head", scatter_dimension=1, tiled=True
    )
    out_dir = contract_cols(lax.all_gather(out_grad, "head", axis=1, tiled=True), full_weight)
    out_dir = out_dir.reshape(length, heads_here, HEAD_DIM)
    along_dir = jnp.mean(out_dir * normed, axis=-1, keepdims=True)
    numer_grad = ((out_dir - normed * along_dir) / spread).astype(jnp.bfloat16)
    local_grad = jnp.einsum(
        "thd,the->hde", query_heads, numer_grad, preferred_element_type=jnp.float32
    )
    suffix = prefix_3(local_grad, "seq", add_states, jnp.zeros_like(local_grad))
    suffix_low = suffix.astype(jnp.bfloat16)
    pair_scores = jnp.einsum(
        "the,she->hts", numer_grad, value_heads, preferred_element_type=jnp.float32
    )
    pair_low = jnp.where(causal, pair_scores, 0.0).astype(jnp.bfloat16)
    query_out = jnp.einsum("hts,shd->thd", pair_low, key_heads, preferred_element_type=jnp.float32)
    query_out = query_out + jnp.einsum(
        "the,hde->thd", numer_grad, prefix_low, preferred_element_type=jnp.float32
    )
    key_out = jnp.einsum("hts,thd->shd", pair_low, query_heads, preferred_element_type=jnp.float32)
    key_out = key_out + jnp.einsum(
        "she,hde->shd", value_heads, suffix_low, preferred_element_type=jnp.float32
    )
    value_out = jnp.einsum("hts,the->she", weights, numer_grad, preferred_element_type=jnp.float32)
    value_out = value_out + jnp.einsum(
        "shd,hde->she", key_heads, suffix_low, preferred_element_type=jnp.float32
    )
    flat_shape = (length, heads_here * HEAD_DIM)
    return (
        layer_out,
        query_out.reshape(flat_shape).astype(jnp.bfloat16),
        key_out.reshape(flat_shape).astype(jnp.bfloat16),
        value_out.reshape(flat_shape).astype(jnp.bfloat16),
    )


def kernel(
    blocks, chunks, parts, q_in, k_in, v_in, w_ref, g_ref,
    mixed_ref, dq_ref, dk_ref, dv_ref,
    q_ref, k_ref, v_ref, w_all, g_all, st_send, prefix, lg_send, suffix, a_buf, b_send, b_buf, c_send,
    out_dir, od_send, od_recv, normed, inv_spread, weights, att, p_own, p_send, p_recv, m_send, m_recv,
    ng, k_part, v_part,
    w_recv_sem, w_send_sem, local_sem, g_send_sem, g_recv_sem,
    a_send_sem, a_recv_sem, b_send_sem, b_recv_sem, c_send_sem, c_recv_sem,
    p_send_sem, p_recv_sem, m_sem, t_sem, o_send_sem, o_recv_sem,
):
    me = lax.axis_index("seq")
    core = lax.axis_index("head")
    other = 1 - core
    planes = blocks // PLANE
    size = blocks // 2
    spot = lax.rem(me, PLANE)
    level = me // PLANE
    bit_x, bit_y = lax.rem(spot, 2), spot // 2
    length, width = q_ref.shape
    heads = width // HEAD_DIM
    rows, cols = w_ref.shape
    chunk = rows // chunks
    chunk_heads = chunk // HEAD_DIM
    lower = level < planes // 2
    middle = jnp.where(lower, level, planes - 1 - level) > 0
    edge = jnp.logical_not(middle)
    nbr_x = me + 1 - 2 * bit_x
    nbr_y = me + 2 - 4 * bit_y
    step_in = jnp.where(lower, PLANE, -PLANE)
    inner = me + step_in
    outer = jnp.where(middle, me - step_in, inner)

    def at_seq(position):
        return (position, core)

    def own_col(k):
        return jnp.where(lower, k, planes - 1 - k) * 2 + bit_y

    def other_col(k):
        return jnp.where(lower, k, planes - 1 - k) * 2 + 1 - bit_y

    o0, o1, o2, o3 = (own_col(k) for k in range(4))
    c0, c1, c2, c3 = (other_col(k) for k in range(4))
    mine = me // 2
    near_own = jnp.where(middle, o0, o1)
    near_other, next_other = jnp.where(middle, c1, c0), jnp.where(middle, c0, c1)
    groups = ((mine, near_own, near_other), (o2, next_other), (o3, c2), (c3,))

    q_load = pltpu.make_async_copy(q_in, q_ref, local_sem.at[0])
    k_load = pltpu.make_async_copy(k_in, k_ref, local_sem.at[1])
    v_load = pltpu.make_async_copy(v_in, v_ref, local_sem.at[2])
    own_w = pltpu.make_async_copy(w_ref, w_all.at[mine], local_sem.at[3])
    k_load.start()
    v_load.start()
    barrier = pltpu.get_barrier_semaphore()

    def greet(i, carry):
        for mate in (level * PLANE + lax.rem(spot + i, PLANE), lax.rem(level + i, planes) * PLANE + spot):
            pl.semaphore_signal(barrier, inc=1, device_id=at_seq(mate), device_id_type=MESH)
        return carry

    lax.fori_loop(1, PLANE, greet, 0)
    pl.semaphore_signal(barrier, inc=1, device_id=(me, other), device_id_type=MESH)

    half = size // 2
    own_rows, far_rows = pl.ds(0, length), pl.ds(length, length)

    def bulk(ref, sent=None, got=None):
        copy = pltpu.make_async_remote_copy(
            src_ref=ref, dst_ref=ref,
            send_sem=got if sent is None else sent, recv_sem=sent if got is None else got,
            device_id=(me, other), device_id_type=MESH,
        )
        copy.wait_recv() if sent is None else copy.wait_send()

    def grad_cols(j, parity):
        return pl.ds(pl.multiple_of((lax.rem(j, half) * 2 + parity) * cols, cols), cols)

    def own_grad(i):
        j = core * half + i
        return pltpu.make_async_copy(g_ref.at[:, grad_cols(j, bit_x)], g_all.at[j, own_rows], local_sem.at[4])

    def grad_core(i):
        j = core * half + i
        return pltpu.make_async_remote_copy(
            src_ref=g_ref.at[:, grad_cols(j, bit_x)], dst_ref=g_all.at[j, own_rows],
            send_sem=g_send_sem.at[0], recv_sem=g_recv_sem.at[0],
            device_id=(me, other), device_id_type=MESH,
        )

    def grad_pair(i):
        j = core * half + i
        return pltpu.make_async_remote_copy(
            src_ref=g_ref.at[:, grad_cols(j, 1 - bit_x)], dst_ref=g_all.at[j, far_rows],
            send_sem=g_send_sem.at[1], recv_sem=g_recv_sem.at[1],
            device_id=at_seq(nbr_x), device_id_type=MESH,
        )

    def grad_relay(i):
        j = core * half + i
        return pltpu.make_async_remote_copy(
            src_ref=g_all.at[j, far_rows], dst_ref=g_all.at[j, far_rows],
            send_sem=g_send_sem.at[2], recv_sem=g_recv_sem.at[2],
            device_id=(me, other), device_id_type=MESH,
        )

    q_load.start()
    own_w.start()
    for i in range(half):
        own_grad(i).start()
    def head_cols(h):
        return pl.ds(pl.multiple_of(h * HEAD_DIM, HEAD_DIM), HEAD_DIM)

    def make_state(h, carry):
        c = head_cols(h)
        st_send[c] = contract_rows(k_ref[:, c], v_ref[:, c]).astype(jnp.bfloat16)
        return carry

    def at_of(kind):
        first, count = (0, chunks) if kind == 0 else (sum(parts[: kind - 1]), parts[kind - 1])
        quarter = count * chunk // PLANE
        return first * chunk, first * chunk // PLANE, quarter

    def a_copy(kind, peer, sender):
        base, packed, quarter = at_of(kind)
        source = st_send if kind == 0 else lg_send
        return pltpu.make_async_remote_copy(
            src_ref=source.at[pl.ds(base + peer * quarter, quarter)],
            dst_ref=a_buf.at[min(kind, 1), sender, pl.ds(packed, quarter)],
            send_sem=a_send_sem.at[kind], recv_sem=a_recv_sem.at[kind],
            device_id=at_seq(level * PLANE + peer), device_id_type=MESH,
        )

    def b_copy(kind, plane, sender):
        packed, quarter = at_of(kind)[1:]
        return pltpu.make_async_remote_copy(
            src_ref=b_send.at[min(kind, 1), pl.ds(packed, quarter)],
            dst_ref=b_buf.at[min(kind, 1), sender, pl.ds(packed, quarter)],
            send_sem=b_send_sem.at[kind], recv_sem=b_recv_sem.at[kind],
            device_id=at_seq(plane * PLANE + spot), device_id_type=MESH,
        )

    def c_copy(kind, peer, sender):
        base, packed, quarter = at_of(kind)
        target = prefix if kind == 0 else suffix
        return pltpu.make_async_remote_copy(
            src_ref=c_send.at[min(kind, 1), peer, pl.ds(packed, quarter)],
            dst_ref=target.at[pl.ds(base + sender * quarter, quarter)],
            send_sem=c_send_sem.at[kind], recv_sem=c_recv_sem.at[kind],
            device_id=at_seq(level * PLANE + peer), device_id_type=MESH,
        )

    def mates(body):
        def one(i, carry):
            body(lax.rem(spot + i, PLANE))
            return carry

        lax.fori_loop(1, PLANE, one, 0)

    def later(kind, body):
        def one(i, carry):
            plane = level + i if kind == 0 else level - planes + i

            @pl.when(jnp.logical_and(plane >= 0, plane < planes))
            def _():
                body(jnp.clip(plane, 0, planes - 1))

            return carry

        lax.fori_loop(1, planes, one, 0)

    def behind(kind):
        return level if kind == 0 else planes - 1 - level

    def rows_for(kind, count):
        return st_send.at[pl.ds(0, count * at_of(kind)[2])]

    def tiles(kind, body):
        packed, quarter = at_of(kind)[1:]

        def one(i, carry):
            body(pl.multiple_of(i * TILE, TILE), pl.ds(pl.multiple_of(packed + i * TILE, TILE), TILE))
            return carry

        lax.fori_loop(0, quarter // TILE, one, 0)

    def own_quarter(kind):
        base, packed, quarter = at_of(kind)
        source = st_send if kind == 0 else lg_send
        a_buf[min(kind, 1), spot, pl.ds(packed, quarter)] = source[pl.ds(base + spot * quarter, quarter)]

    def scan_open(kind):
        mates(lambda peer: a_copy(kind, peer, spot).start())
        own_quarter(kind)

    def scan_planes(kind):
        way = min(kind, 1)
        bulk(rows_for(kind, PLANE - 1), got=a_recv_sem.at[kind])

        def tile(_, here):
            total = a_buf[way, 0, here].astype(jnp.float32)
            for s in range(1, PLANE):
                total = total + a_buf[way, s, here].astype(jnp.float32)
            b_send[way, here] = total.astype(jnp.bfloat16)

        tiles(kind, tile)
        later(kind, lambda plane: b_copy(kind, plane, level).start())

    def scan_close(kind):
        base, packed, quarter = at_of(kind)
        way = min(kind, 1)
        target = prefix if kind == 0 else suffix
        for count in range(1, planes):

            @pl.when(behind(kind) == count)
            def _():
                bulk(rows_for(kind, count), got=b_recv_sem.at[kind])


        def tile(_, here):
            total = b_buf[way, 0, here].astype(jnp.float32)
            for z in range(1, planes):
                total = total + b_buf[way, z, here].astype(jnp.float32)
            for s in range(PLANE) if kind == 0 else range(PLANE - 1, -1, -1):
                c_send[way, s, here] = total.astype(jnp.bfloat16)
                total = total + a_buf[way, s, here].astype(jnp.float32)

        tiles(kind, tile)
        mates(lambda peer: c_copy(kind, peer, spot).start())
        target[pl.ds(base + spot * quarter, quarter)] = c_send[way, spot, pl.ds(packed, quarter)]

    def scan_end(kind):
        bulk(rows_for(kind, PLANE - 1), got=c_recv_sem.at[kind])

    def scan_sent(kind):
        bulk(rows_for(kind, PLANE - 1), sent=a_send_sem.at[kind])
        bulk(rows_for(kind, PLANE - 1), sent=c_send_sem.at[kind])
        for count in range(1, planes):

            @pl.when(planes - 1 - behind(kind) == count)
            def _():
                bulk(rows_for(kind, count), sent=b_send_sem.at[kind])

    def span_of(c):
        return pl.ds(pl.multiple_of(c * chunk, chunk), chunk)

    def piece(j, c, sems, target, own=False):
        span = span_of(c)
        return pltpu.make_async_remote_copy(
            src_ref=w_ref.at[span] if own else w_all.at[j, span],
            dst_ref=w_all.at[j, span],
            send_sem=sems, recv_sem=w_recv_sem.at[j, c],
            device_id=at_seq(target), device_id_type=MESH,
        )

    def to_y(j, c, own=False, slot=0):
        return piece(j, c, w_send_sem.at[slot], nbr_y, own)

    def to_inner(j, c, own=False):
        return piece(j, c, w_send_sem.at[1], inner, own)

    def to_outer(j, c, own=False, slot=2):
        return piece(j, c, w_send_sem.at[slot], outer, own)

    def landed(j, c):
        to_y(j, c).wait_recv()

    def own_piece(c):
        to_y(mine, c, True).start()
        to_inner(mine, c, True).start()

        @pl.when(middle)
        def _():
            to_outer(mine, c, True).start()

    turns = 0, parts[0], parts[0] + parts[1]

    def by_y(c):
        return jnp.logical_or(c == turns[0], jnp.logical_or(c == turns[1], c == turns[2]))

    def pump(phase, c):
        def move(j, ways):
            landed(j, c)
            for way in ways:
                way(j, c).start()

        if phase == 0:

            @pl.when(edge)
            def _():
                move(c0, (to_inner,))
                move(o1, (to_y,))

            @pl.when(middle)
            def _():
                move(o0, (to_inner,))
                move(o2, (to_outer, to_y))

        elif phase == 1:

            @pl.when(edge)
            def _():
                move(o2, (to_y,))

            @pl.when(middle)
            def _():
                move(o3, (to_outer, to_y))

        else:

            @pl.when(edge)
            def _():
                landed(o3, c)

                @pl.when(by_y(c))
                def _():
                    to_y(o3, c, slot=3).start()

            @pl.when(middle)
            def _():
                landed(c3, c)

                @pl.when(jnp.logical_not(by_y(c)))
                def _():
                    to_outer(c3, c, slot=3).start()

    def pieces_sent():
        bulk(w_all.at[pl.ds(0, 3)], sent=w_send_sem.at[0])
        bulk(w_all.at[pl.ds(0, 2)], sent=w_send_sem.at[1])

        @pl.when(middle)
        def _():
            bulk(w_all.at[pl.ds(0, 3)], sent=w_send_sem.at[2])
            bulk(w_all.at[0, pl.ds(0, (chunks - len(turns)) * chunk)], sent=w_send_sem.at[3])

        @pl.when(edge)
        def _():
            bulk(w_all.at[0, pl.ds(0, len(turns) * chunk)], sent=w_send_sem.at[3])

    def settle(group, c):
        if group == 0:

            @pl.when(middle)
            def _():
                landed(c1, c)

        elif group == 1:
            landed(next_other, c)
        elif group == 2:
            landed(c2, c)
        else:

            @pl.when(edge)
            def _():
                landed(c3, c)

    causal = lower_mask(length)

    def score_step(h, carry):
        c = head_cols(h)
        kept = jnp.where(causal, contract_cols(q_ref[:, c], k_ref[:, c]), 0.0).astype(jnp.bfloat16)
        weights[h] = kept
        normed[h] = contract_mid(kept, v_ref[:, c])
        return carry

    def norm_step(h, carry):
        c = head_cols(h)
        numerator = normed[h] + contract_mid(q_ref[:, c], prefix[c])
        inv = 1.0 / jnp.sqrt(jnp.mean(numerator * numerator, axis=-1, keepdims=True) + 1e-06)
        value = numerator * inv
        normed[h] = value
        inv_spread[h] = jnp.broadcast_to(inv, (length, HEAD_DIM))
        att[own_rows, c] = value.astype(jnp.bfloat16)
        return carry

    def att_copy(i):
        c = span_of(i)
        return pltpu.make_async_remote_copy(
            src_ref=att.at[own_rows, c], dst_ref=att.at[far_rows, c],
            send_sem=t_sem.at[0], recv_sem=t_sem.at[1],
            device_id=at_seq(nbr_x), device_id_type=MESH,
        )

    def od_copy(c):
        return pltpu.make_async_remote_copy(
            src_ref=od_send.at[c], dst_ref=od_recv.at[c],
            send_sem=o_send_sem.at[0], recv_sem=o_recv_sem.at[c],
            device_id=at_seq(nbr_x), device_id_type=MESH,
        )

    def direction_step(group, c):
        span = span_of(c)
        total = None
        for j in groups[group]:
            term = contract_cols(g_all[j], w_all[j, span])
            total = term if total is None else total + term
        if group > 0:
            total = total + out_dir[:, span]
        if group < len(groups) - 1:
            out_dir[:, span] = total
        else:
            out_dir[own_rows, span] = total[:length]
            od_send[c] = total[length:].astype(jnp.bfloat16)
            od_copy(c).start()

    def p_copy(slot):
        return pltpu.make_async_remote_copy(
            src_ref=p_send.at[slot], dst_ref=p_recv.at[slot],
            send_sem=p_send_sem.at[0], recv_sem=p_recv_sem.at[slot],
            device_id=(me, other), device_id_type=MESH,
        )

    def m_copy(slot):
        return pltpu.make_async_remote_copy(
            src_ref=m_send.at[slot], dst_ref=m_recv.at[slot],
            send_sem=m_sem.at[0], recv_sem=m_sem.at[1],
            device_id=at_seq(nbr_x), device_id_type=MESH,
        )

    def partial_step(j):
        term = contract_mid(att[...], w_all[j]).astype(jnp.bfloat16)
        slot = lax.rem(j, half)

        @pl.when(j // half == core)
        def _():
            p_own[slot] = term

        @pl.when(j // half != core)
        def _():
            p_send[slot] = term
            p_copy(slot).start()

    def mixed_cols(slot, parity):
        return pl.ds(pl.multiple_of((slot * 2 + parity) * cols, cols), cols)

    def mix_step(slot, carry):
        p_copy(slot).wait_recv()
        both = (p_own[slot].astype(jnp.float32) + p_recv[slot].astype(jnp.float32)).astype(jnp.bfloat16)
        m_send[slot] = both[length:]
        m_copy(slot).start()
        mixed_ref[:, mixed_cols(slot, bit_x)] = both[:length]
        return carry

    def numer_step(h, carry):
        c = head_cols(h)
        sub = pl.ds(pl.multiple_of(lax.rem(h, chunk_heads) * HEAD_DIM, HEAD_DIM), HEAD_DIM)
        toward = out_dir[own_rows, c] + od_recv[h // chunk_heads, :, sub].astype(jnp.float32)
        unit = normed[h]
        along = jnp.mean(toward * unit, axis=-1, keepdims=True)
        low = ((toward - unit * along) * inv_spread[h]).astype(jnp.bfloat16)
        ng[:, c] = low
        lg_send[c] = contract_rows(q_ref[:, c], low).astype(jnp.bfloat16)
        return carry

    def numer_chunk(c):
        od_copy(c).wait_recv()
        lax.fori_loop(c * chunk_heads, (c + 1) * chunk_heads, numer_step, 0)

    def pair_step(h, carry):
        c = head_cols(h)
        low = ng[:, c]
        pair = jnp.where(causal, contract_cols(low, v_ref[:, c]), 0.0).astype(jnp.bfloat16)
        dq_ref[:, c] = (contract_mid(pair, k_ref[:, c]) + contract_cols(low, prefix[c])).astype(jnp.bfloat16)
        k_part[h] = contract_rows(pair, q_ref[:, c])
        v_part[h] = contract_rows(weights[h], low)
        return carry

    def each(count, body):
        def one(i, carry):
            body(i)
            return carry

        lax.fori_loop(0, count, one, 0)

    def heads_of(c, body):
        lax.fori_loop(c * chunk_heads, (c + 1) * chunk_heads, body, 0)

    def last_step(h, carry):
        c = head_cols(h)
        dk_ref[:, c] = (k_part[h] + contract_cols(v_ref[:, c], suffix[c])).astype(jnp.bfloat16)
        dv_ref[:, c] = (v_part[h] + contract_mid(k_ref[:, c], suffix[c])).astype(jnp.bfloat16)
        return carry

    def each(first, last, body):
        def one(i, carry):
            body(i)
            return carry

        lax.fori_loop(first, last, one, 0)

    def aim(group, first, last):
        def one(c):
            settle(group, c)
            direction_step(group, c)

        each(first, last, one)

    e1, e2, e3 = parts[0], parts[0] + parts[1], chunks

    pl.semaphore_wait(barrier, 2 * PLANE - 1)
    own_piece(0)
    for i in range(half):
        grad_core(i).start()
    grad_pair(0).start()
    for z in range(planes):

        @pl.when(z >= level)
        def _():
            b_buf[0, z] = jnp.zeros(b_buf.shape[2:], b_buf.dtype)

        @pl.when(z <= level)
        def _():
            b_buf[1, z] = jnp.zeros(b_buf.shape[2:], b_buf.dtype)

    k_load.wait()
    v_load.wait()
    team = heads // PLANE

    def some_states(peer):
        lax.fori_loop(peer * team, (peer + 1) * team, make_state, 0)

    def open_states(peer):
        some_states(peer)
        a_copy(0, peer, spot).start()

    mates(open_states)
    each(1, half, lambda i: grad_pair(i).start())
    each(1, e1, own_piece)
    some_states(spot)
    own_quarter(0)
    q_load.wait()
    lax.fori_loop(0, heads, score_step, 0)
    scan_planes(0)
    pump(0, 0)
    scan_close(0)
    each(1, e1, lambda c: pump(0, c))
    each(0, e1, lambda c: pump(1, c))
    each(e1, e2, own_piece)
    some_grads = g_all.at[pl.ds(0, half), own_rows]
    bulk(some_grads, got=g_recv_sem.at[1])
    for i in range(half):
        grad_relay(i).start()
    own_w.wait()
    pltpu.make_async_copy(some_grads, some_grads, local_sem.at[4]).wait()
    bulk(some_grads, got=g_recv_sem.at[0])
    scan_end(0)

    def stage(c):
        heads_of(c, norm_step)
        att_copy(c).start()

    each(0, 4, stage)
    each(0, e1, lambda c: pump(2, c))
    bulk(some_grads, got=g_recv_sem.at[2])
    each(4, chunks, lambda c: heads_of(c, norm_step))
    aim(0, 0, e1)
    aim(1, 0, e1)
    aim(2, 0, e1)
    aim(3, 0, e1)

    def stage(c):
        pump(0, c)
        att_copy(c - e1 + 4).start()

    each(e1, e2, stage)
    each(e2, e3, own_piece)
    each(e2 - e1 + 4, chunks, lambda c: att_copy(c).start())
    each(0, e1, numer_chunk)
    scan_open(1)
    each(e2, e3, lambda c: pump(0, c))

    def stage(c):
        pump(1, c)
        settle(0, c)
        direction_step(0, c)
        heads_of(c - e1, pair_step)

    each(e1, e2, stage)
    scan_planes(1)
    bulk(att.at[own_rows], got=t_sem.at[1])
    aim(0, e2, e3)
    partial_step(mine)
    partial_step(near_own)
    partial_step(near_other)
    aim(1, e1, e2)
    each(e2, e3, lambda c: settle(1, c))
    partial_step(next_other)
    pump(2, e1)
    near = level // (planes // 2)

    @pl.when(core == near)
    def _():
        lax.fori_loop(0, half, mix_step, 0)

    each(e1 + 1, e2 - 1, lambda c: pump(2, c))
    scan_close(1)
    each(e2 - 1, e2, lambda c: pump(2, c))
    each(e2, e3, lambda c: pump(1, c))
    each(e2, e3, lambda c: direction_step(1, c))
    partial_step(o2)
    aim(2, e1, e2)
    aim(3, e1, e2)
    each(e2, e3, lambda c: pump(2, c))
    aim(2, e2, e3)
    partial_step(o3)
    aim(3, e2, e3)
    each(e1, e2, numer_chunk)
    scan_open(2)
    partial_step(c2)
    scan_end(1)
    each(0, e1, lambda c: heads_of(c, last_step))
    each(e1, e2, lambda c: heads_of(c, pair_step))

    def far_mix(*blocks_done):
        @pl.when(core != near)
        def _():
            for j in blocks_done:
                mix_step(lax.rem(j, half), 0)

    each(e2, e3, numer_chunk)
    scan_open(3)
    far_mix(o2, o3)
    partial_step(c3)
    scan_planes(2)
    scan_planes(3)

    @pl.when(level == planes - 1)
    def _():
        scan_close(2)
        scan_close(3)

    far_mix(c2, c3)
    each(e2, e3, lambda c: heads_of(c, pair_step))
    @pl.when(level < planes - 1)
    def _():
        scan_close(2)
        scan_close(3)

    scan_end(2)
    each(e1, e2, lambda c: heads_of(c, last_step))
    scan_end(3)
    each(e2, e3, lambda c: heads_of(c, last_step))

    def take_mixed(slot, carry):
        mixed_ref[:, mixed_cols(slot, 1 - bit_x)] = m_recv[slot]
        return carry

    bulk(m_recv, got=m_sem.at[1])
    lax.fori_loop(0, half, take_mixed, 0)

    pieces_sent()
    bulk(od_send, sent=o_send_sem.at[0])
    bulk(att.at[own_rows], sent=t_sem.at[0])
    bulk(p_send, sent=p_send_sem.at[0])
    bulk(m_send, sent=m_sem.at[0])
    for i in range(3):
        bulk(some_grads, sent=g_send_sem.at[i])
    for kind in range(len(parts) + 1):
        scan_sent(kind)


def store_kernel(*refs):
    count = (len(refs) - 1) // 2
    copies = [pltpu.make_async_copy(refs[i], refs[count + i], refs[-1].at[i]) for i in range(count)]
    for copy in copies:
        copy.start()
    for copy in copies:
        copy.wait()


def store(*arrays):
    count = len(arrays)
    return pl.pallas_call(
        store_kernel,
        out_shape=tuple(jax.ShapeDtypeStruct(a.shape, a.dtype) for a in arrays),
        in_specs=[pl.BlockSpec(memory_space=pltpu.VMEM)] * count,
        out_specs=(pl.BlockSpec(memory_space=pltpu.HBM),) * count,
        scratch_shapes=[pltpu.SemaphoreType.DMA((count,))],
        compiler_params=pltpu.CompilerParams(vmem_limit_bytes=8 * 2**20),
    )(*arrays)


def fused(blocks, queries, key_rows, values, out_weight, out_grad):
    length, width = queries.shape
    heads = width // HEAD_DIM
    rows, cols = out_weight.shape
    low, wide = jnp.bfloat16, jnp.float32
    size = blocks // 2
    half = size // 2
    chunks = sum(PARTS)
    state = pltpu.VMEM((rows, HEAD_DIM), low)
    fourth = rows // PLANE
    by_spot = pltpu.VMEM((2, PLANE, fourth, HEAD_DIM), low)
    by_head = pltpu.VMEM((heads, length, HEAD_DIM), wide)
    flat = pltpu.VMEM((length, width), low)
    parts = pltpu.VMEM((half, 2 * length, cols), low)
    shares = pltpu.VMEM((half, length, cols), low)
    steps = pltpu.VMEM((chunks, length, rows // chunks), low)
    dma = pltpu.SemaphoreType.DMA
    out = jax.ShapeDtypeStruct((length, width), low)
    vmem, in_hbm = pl.BlockSpec(memory_space=pltpu.VMEM), pl.BlockSpec(memory_space=pltpu.HBM)
    scans = dma((len(PARTS) + 1,))
    results = pl.pallas_call(
        functools.partial(kernel, blocks, chunks, PARTS),
        out_shape=(out, out, out, out),
        in_specs=[in_hbm] * 5,
        out_specs=(vmem, vmem, vmem, vmem),
        scratch_shapes=[
            flat, flat, flat,
            pltpu.VMEM((size, rows, cols), low),
            pltpu.VMEM((size, 2 * length, cols), low),
            state, state, state, state,
            by_spot, pltpu.VMEM((2, fourth, HEAD_DIM), low), by_spot, by_spot,
            pltpu.VMEM((2 * length, rows), wide),
            steps, steps,
            by_head, by_head,
            pltpu.VMEM((heads, length, length), low),
            pltpu.VMEM((2 * length, width), low),
            parts, parts, parts, shares, shares,
            flat, by_head, by_head,
            dma((size, chunks)), dma((4,)), dma((5,)), dma((3,)), dma((3,)),
            scans, scans, scans, scans, scans, scans,
            dma((1,)), dma((half,)), dma((2,)), dma((2,)), dma((1,)), dma((chunks,)),
        ],
        compiler_params=pltpu.CompilerParams(
            collective_id=0, has_side_effects=True, vmem_limit_bytes=49 * 2**20
        ),
    )(queries, key_rows, values, out_weight, out_grad)
    return store(*results)


def solution(mesh):
    blocks, cores = mesh.shape["seq"], mesh.shape["head"]

    def step(queries, key_rows, values, out_weight, out_grad):
        heads = queries.shape[1] // HEAD_DIM
        fits = cores == 2 and blocks == PLANE * PLANE and heads == blocks and out_weight.shape[1] % HEAD_DIM == 0
        fits = fits and out_weight.shape[0] == queries.shape[1] and out_weight.shape[0] % out_weight.shape[1] == 0
        if fits and out_weight.shape[1] * blocks == queries.shape[1] * cores:
            return fused(blocks, queries, key_rows, values, out_weight, out_grad)
        return per_device(queries, key_rows, values, out_weight, out_grad)

    placed = (
        P("seq", "head"),
        P("seq", "head"),
        P("seq", "head"),
        P("head", "seq"),
        P("seq", "head"),
    )
    return jax.shard_map(
        step,
        mesh=mesh,
        in_specs=placed,
        out_specs=(P("seq", "head"), P("seq", "head"), P("seq", "head"), P("seq", "head")),
        check_vma=False,
    )
```
